32 devices in a mesh: grp: 2 (over y), lat: 4 (over z), chan: 2 (over core), ens: 2 (over x).
Axes of the slice: x: 2, y: 2, z: 4, core: 2. Of those that a mesh axis runs over, the one named last changes fastest.
Arguments:
- grad_out: bfloat16 [4, 24, 48, 384], P(('grp', 'ens'), 'lat', None, 'chan'), parts along dimension 0, may hold values from -6 to 6
- pre_act: bfloat16 [4, 24, 48, 384], P(('grp', 'ens'), 'lat', None, 'chan'), parts along dimension 0, may hold values from -6 to 6
- coeffs: bfloat16 [4, 24, 24, 2, 384], P(('grp', 'ens'), ('lat', 'chan')), parts along dimension 0, may hold values from -6 to 6
- legendre: bfloat16 [24, 24, 24], P(('lat', 'chan'), None, 'ens'), may hold values from -1.25 to 1.25
- mixing: bfloat16 [384, 384], replicated, may hold values from -0.3125 to 0.3125
Outputs:
- grad_in: bfloat16 [4, 24, 48, 384], P(('grp', 'ens'), 'lat', None, 'chan'), parts along dimension 0
- mixing_grad: float32 [768, 384], P('grp'), parts along dimension 0
The draws below stay inside these ranges and needn't reach their ends.
There are 2 independent parts, one for each index of `grp`. The reference program is written for one: setup_inputs(seed, part) draws one part's arguments, and reference() takes and returns one part's arrays. A program takes and returns all parts, laid end to end along the dimension named above; an argument that names none is the same for every part. Nothing has to cross between parts.
All inputs are finite; a program needn't handle non-finite values.
Results may differ from the reference program's by a relative error of at most 0.0074.
Values may be sent and summed in bfloat16 or wider, within the bound.
A program may use at most 64 MiB of HBM per device.

```python
import math
import jax
import jax.numpy as jnp
from jax import lax

C = 384
NLAT = 24
NLON = 48
MODES = 24
DEGREES = 24
ENS = 2


def block_scale(key, extent, cuts, low, top_value):
    loudness, own = 1.0, jax.random.fold_in(key, 6)
    for position, shards_of in cuts:
        steps = jnp.exp(jax.random.uniform(jax.random.fold_in(own, position), (shards_of,), jnp.float32, low / len(cuts), top_value / len(cuts)))
        loudness = loudness * jnp.repeat(steps, extent[position] // shards_of).reshape([-1 if axis == position else 1 for axis in range(len(extent))])
    return loudness


def gaussian(stream_key, dims, scale, bound, pieces=(), kind=jnp.bfloat16):
    values = jax.random.normal(stream_key, dims, jnp.float32) * scale
    if len(pieces) > 0:
        values = block_scale(stream_key, dims, pieces, -0.22, 0.18) * values
    return jnp.clip(values, min=-bound, max=bound).astype(kind)


def setup_inputs(seed: int = 0, part: int = 0) -> dict:
    splits = jax.random.split(jax.random.key(seed), 6)
    part_splits = jax.random.split(jax.random.fold_in(splits[5], part), 6)
    grad_out = gaussian(part_splits[0], (ENS, NLAT, NLON, C), 1.0, 6.0, ((0, 2), (1, 4), (3, 2)))
    pre_act = gaussian(part_splits[1], (ENS, NLAT, NLON, C), 1.5, 6.0, ((0, 2), (1, 4), (3, 2)))
    coeffs = gaussian(part_splits[2], (ENS, MODES, DEGREES, 2, C), 1.0, 6.0, ((0, 2), (1, 8)))
    legendre = gaussian(splits[3], (MODES, DEGREES, NLAT), NLAT ** -0.5, 1.25, ((0, 8), (2, 2)))
    mixing = gaussian(splits[4], (C, C), C ** -0.5, 0.3125)
    return dict(grad_out=grad_out, pre_act=pre_act, coeffs=coeffs, legendre=legendre, mixing=mixing)


def fourier_table(lon_count, mode_count):
    longitude = jnp.arange(lon_count, dtype=jnp.int32)[:, None]
    wavenumber = jnp.arange(mode_count, dtype=jnp.int32)[None, :]
    product_index = longitude * wavenumber % lon_count
    angles = 2.0 * math.pi / lon_count * product_index.astype(jnp.float32)
    factor = math.sqrt(2.0 / lon_count)
    stacked = jnp.stack([jnp.cos(angles), -jnp.sin(angles)], axis=2) * factor
    return stacked.reshape(lon_count, 2 * mode_count).astype(jnp.bfloat16)

def silu_backward(cotangent, preact):
    values = preact.astype(jnp.float32)
    gate_value = jax.nn.sigmoid(values)
    return (cotangent.astype(jnp.float32) * gate_value * (1.0 + values * (1.0 - gate_value))).astype(jnp.bfloat16)

def reference(grad_out, pre_act, coeffs, legendre, mixing):
    fourier = fourier_table(NLON, MODES)
    fourier_wide = fourier.astype(jnp.float32)
    legendre_wide = legendre.astype(jnp.float32)
    weight_scale = 1.0 / (ENS * MODES)

    def member(member_data):
        cotangent, preact, stored = member_data
        scaled = silu_backward(cotangent, preact)
        spectral = jnp.einsum('nk,anc->akc', fourier_wide, scaled.astype(jnp.float32)).astype(jnp.bfloat16)
        spectral = spectral.reshape(NLAT, MODES, 2, C)
        coef_grad = jnp.einsum('mla,amrc->mlrc', legendre_wide, spectral.astype(jnp.float32)).astype(jnp.bfloat16)
        flat_grad = coef_grad.reshape(-1, C)
        weight_grad = jnp.dot(stored.reshape(-1, C).T, flat_grad, preferred_element_type=jnp.float32) * weight_scale
        mixed_grad = jnp.dot(flat_grad, mixing.T, preferred_element_type=jnp.float32).astype(jnp.bfloat16)
        mixed_grad = mixed_grad.reshape(MODES, DEGREES, 2, C)
        returned = jnp.einsum('mla,mlrc->amrc', legendre_wide, mixed_grad.astype(jnp.float32)).astype(jnp.bfloat16)
        returned = returned.reshape(NLAT, 2 * MODES, C)
        spatial = jnp.einsum('nk,akc->anc', fourier_wide, returned.astype(jnp.float32))
        result = (cotangent.astype(jnp.float32) + spatial).astype(jnp.bfloat16)
        return (result, weight_grad)
    results, weight_grads = lax.map(member, (grad_out, pre_act, coeffs))
    return (results, lax.optimization_barrier(jnp.sum(weight_grads, axis=0)))
```

```python
import math

import jax
import jax.numpy as jnp
import numpy as np
from jax import lax
from jax.experimental import pallas as pl
from jax.experimental.pallas import tpu as pltpu
from jax.sharding import PartitionSpec as P


def fourier_table(lon_count, mode_count):
    longitude = jnp.arange(lon_count, dtype=jnp.int32)[:, None]
    wavenumber = jnp.arange(mode_count, dtype=jnp.int32)[None, :]
    product_index = longitude * wavenumber % lon_count
    angles = 2.0 * math.pi / lon_count * product_index.astype(jnp.float32)
    factor = math.sqrt(2.0 / lon_count)
    stacked = jnp.stack([jnp.cos(angles), -jnp.sin(angles)], axis=2) * factor
    return stacked.reshape(lon_count, 2 * mode_count).astype(jnp.bfloat16)


def silu_backward(cotangent, preact):
    values = preact.astype(jnp.float32)
    gate_value = jax.nn.sigmoid(values)
    return (
        cotangent.astype(jnp.float32) * gate_value * (1.0 + values * (1.0 - gate_value))
    ).astype(jnp.bfloat16)


def on_device(grad_out, pre_act, coeffs, legendre, mixing):
    lat_rows = grad_out.shape[1]
    lon_count = grad_out.shape[2]
    chan_cols = grad_out.shape[3]
    mode_count = lon_count // 2
    lat_devices = lax.axis_size("lat")
    chan_count = lax.axis_size("chan")
    members = lax.axis_size("ens")
    lat_count = lat_rows * lat_devices
    channels = chan_cols * chan_count
    mode_width = 2 * mode_count // (lat_devices * chan_count)
    local_modes = mode_width // 2
    fourier = fourier_table(lon_count, mode_count)
    scaled = silu_backward(grad_out[0], pre_act[0])
    spectral = jnp.einsum(
        "nk,anc->akc", fourier, scaled, preferred_element_type=jnp.float32
    ).astype(jnp.bfloat16)
    exchanged = lax.all_to_all(
        lax.all_to_all(spectral, "lat", split_axis=1, concat_axis=0, tiled=True),
        "chan",
        split_axis=1,
        concat_axis=2,
        tiled=True,
    )
    spectral_modes = exchanged.reshape(lat_count, local_modes, 2, channels)
    legendre_full = lax.all_gather(legendre, "ens", axis=2, tiled=True)
    coef_grad = jnp.einsum(
        "mla,amrc->mlrc", legendre_full, spectral_modes, preferred_element_type=jnp.float32
    ).astype(jnp.bfloat16)
    stored = coeffs[0].reshape(-1, channels)
    flat_grad = coef_grad.reshape(-1, channels)
    weight_grad = lax.dot_general(
        stored, flat_grad, (((0,), (0,)), ((), ())), preferred_element_type=jnp.float32
    )
    weight_grad = weight_grad * (1.0 / (members * mode_count))
    weight_grad = lax.psum(weight_grad, ("lat", "chan", "ens"))
    mixed_grad = lax.dot_general(
        coef_grad, mixing, (((3,), (1,)), ((), ())), preferred_element_type=jnp.float32
    ).astype(jnp.bfloat16)
    returned = jnp.einsum(
        "mla,mlrc->amrc", legendre_full, mixed_grad, preferred_element_type=jnp.float32
    ).astype(jnp.bfloat16)
    shaped = returned.reshape(lat_count, 1, mode_width, channels)
    received = lax.all_to_all(
        lax.all_to_all(shaped, "lat", split_axis=0, concat_axis=1, tiled=True),
        "chan",
        split_axis=3,
        concat_axis=2,
        tiled=True,
    )
    row_coeffs = received.reshape(lat_rows, 2 * mode_count, chan_cols)
    spatial = jnp.einsum("nk,akc->anc", fourier, row_coeffs, preferred_element_type=jnp.float32)
    result = (grad_out[0].astype(jnp.float32) + spatial).astype(jnp.bfloat16)
    return (result[None], weight_grad)

MESH = pl.DeviceIdType.MESH
BF16 = jnp.bfloat16
F32 = jnp.float32


def dot(a, b, dims=((1,), (0,))):
    return lax.dot_general(a, b, (dims, ((), ())), preferred_element_type=F32)


LANES = 128


def slots(rows, width):
    whole = [(a, a, k) for a in range(rows) for k in range(width)]
    paired = [(a, a + 1, k) for a in range(0, rows, 2) for k in range(width)]
    return whole, paired


def padded(rows, width):
    return -(-(rows + rows // 2) * width // 16) * 16


def tables(rows, lon, lats, chans, members, modes, degrees):
    owners = lats * chans
    width = 2 * modes
    pad = padded(rows, width)
    n = np.arange(lon)[:, None]
    m = np.arange(lon // 2)[None, :]
    angles = np.float32(2.0 * math.pi / lon) * (n * m % lon).astype(np.float32)
    table = np.stack([np.cos(angles), -np.sin(angles)], axis=2).reshape(lon, lon)
    table = (table * np.float32(math.sqrt(2.0 / lon))).astype(np.float32)
    groups = rows + rows // 2
    inverse = np.zeros((groups, lon, owners, pad), np.float32)
    for g in range(groups):
        for d in range(owners):
            inverse[g, :, d, g * width:(g + 1) * width] = table[:, d * width:(d + 1) * width]
    inverse = inverse.reshape(groups * lon, owners * pad)
    whole, paired = slots(rows, width)
    lat_of = np.full((3, lats, pad), -1)
    key_of = np.full((3, lats, pad), -1)
    for z in range(lats):
        for i, (even, odd, k) in enumerate(whole + paired):
            if i < len(whole):
                lat_of[0, z, i], key_of[0, z, i] = z * rows + even, k
            else:
                lat_of[1, z, i], key_of[1, z, i] = z * rows + even, k
                lat_of[2, z, i], key_of[2, z, i] = z * rows + odd, k
    lat_of, key_of = lat_of.reshape(-1), key_of.reshape(-1)
    held = rows * lats // members
    select = (lat_of[None, :] == np.arange(members * held)[:, None]).astype(np.float32)
    select = select.reshape(members, held, -1)
    row = np.arange(modes * degrees * 2)
    spread = (row[:, None] // 2 == np.arange(modes * degrees)[None, :]).astype(np.float32)
    row_key = row // (2 * degrees) * 2 + row % 2
    mask = (row_key[:, None] == key_of[None, :]).astype(np.float32)
    cast = lambda x: jnp.asarray(np.ascontiguousarray(x), BF16)
    return (
        cast(inverse.T), cast(inverse), cast(select), cast(select.transpose(0, 2, 1)),
        cast(spread), cast(spread.T), cast(mask), cast(mask.T),
    )


def fused_kernel(
    lats, chans, members, lon,
    grad_hbm, pre_hbm, coeffs_hbm, leg_hbm, mix_hbm,
    fwd_hbm, inv_hbm, sel_hbm, selt_hbm, spread_hbm, spreadt_hbm, mask_hbm, maskt_hbm,
    out_ref, weight_ref,
    full_ref,
    grad_ref, pre_ref, coeffs_ref, leg_ref, mix_ref,
    fwd_ref, inv_ref, sel_ref, selt_ref, spread_ref, spreadt_ref, mask_ref, maskt_ref,
    stored, lbuf, sbuf, rbuf, sbuf2, rbuf2, w1s, w1r, w2own, w2s, w2r,
    isem, lsem, esem, fsem, r1sem, r2sem, g1sem, g2sem,
):
    z, c, x = lax.axis_index("lat"), lax.axis_index("chan"), lax.axis_index("ens")
    owners, quads = lats * chans, members * chans
    me, quad = z * chans + c, x * chans + c
    pad, cols, blocks = rbuf.shape[2], grad_ref.shape[1], lats * rbuf.shape[2]

    def owner_peer(p):
        q = lax.rem(me + p, owners)
        return q, q // chans, lax.rem(q, chans)

    def quad_peer(p):
        q = lax.rem(quad + p, quads)
        return q, q // chans, lax.rem(q, chans)

    sources = (
        pre_hbm, grad_hbm, fwd_hbm, leg_hbm, sel_hbm, selt_hbm, spread_hbm, spreadt_hbm,
        mask_hbm, maskt_hbm, coeffs_hbm, mix_hbm, inv_hbm,
    )
    targets = (
        pre_ref, grad_ref, fwd_ref, leg_ref, sel_ref, selt_ref, spread_ref, spreadt_ref,
        mask_ref, maskt_ref, coeffs_ref, mix_ref, inv_ref,
    )
    loads = [
        pltpu.make_async_copy(source, target, isem.at[i])
        for i, (source, target) in enumerate(zip(sources, targets))
    ]
    for load in loads:
        load.start()
    barrier = pltpu.get_barrier_semaphore()
    for p in range(1, owners):
        _, pz, pc = owner_peer(p)
        pl.semaphore_signal(barrier, inc=1, device_id={"lat": pz, "chan": pc}, device_id_type=MESH)
    for p in range(1, members):
        for pc in range(chans):
            target = {"ens": lax.rem(x + p, members), "chan": pc}
            pl.semaphore_signal(barrier, inc=1, device_id=target, device_id_type=MESH)

    for load in loads[:4]:
        load.wait()
    values = pre_ref[...].astype(F32)
    gate = jax.nn.sigmoid(values)
    scaled = grad_ref[...].astype(F32) * gate * (1.0 + values * (1.0 - gate))
    points, half = scaled.shape[0], LANES // 2
    tail = scaled[:, LANES:].reshape(-1, 2, lon, half)
    paired = jnp.concatenate([tail[:, 0], tail[:, 1]], axis=-1).reshape(-1, LANES)
    packed = jnp.concatenate([scaled[:, :LANES], paired], axis=0).astype(BF16)
    sbuf[...] = dot(fwd_ref[...], packed).astype(BF16).reshape(owners, pad, LANES)

    pl.semaphore_wait(barrier, owners - 1 + (members - 1) * chans)

    def remote(src, dst, sems, target):
        return pltpu.make_async_remote_copy(
            src_ref=src, dst_ref=dst, send_sem=sems[0], recv_sem=sems[1],
            device_id=target, device_id_type=MESH,
        )

    def pair(sem, *index):
        return sem.at[(0,) + index], sem.at[(1,) + index]

    legs = remote(leg_ref, lbuf, pair(lsem, 0), {"ens": lax.rem(x + 1, members)})
    legs.start()
    started = [legs]
    first = []
    for p in range(1, owners):
        q, pz, pc = owner_peer(p)
        copy = remote(sbuf.at[q], rbuf.at[c, z], pair(esem, p - 1), {"lat": pz, "chan": pc})
        copy.start()
        first.append(copy)
    started += first
    for load in loads[4:]:
        load.wait()
    rbuf[c, z] = sbuf[me]
    legs.wait_recv()
    other = lax.rem(x + 1, members)
    modes, degrees = leg_ref.shape[0], leg_ref.shape[2]
    by_lat, synthesis = [], 0.0
    for m in range(modes):
        mine, theirs = leg_ref[m], lbuf[m]
        down = ((0,), (0,))
        by_lat.append(dot(mine, sel_ref[x], down) + dot(theirs, sel_ref[other], down))
        by_row = dot(selt_ref[x], mine) + dot(selt_ref[other], theirs)
        rows = spreadt_ref[m * degrees:(m + 1) * degrees, :]
        synthesis = synthesis + dot(by_row.astype(BF16), rows)
    by_lat = jnp.concatenate(by_lat, axis=0).astype(BF16)
    analysis = (dot(spread_ref[...], by_lat) * mask_ref[...].astype(F32)).astype(BF16)
    synthesis = (synthesis * maskt_ref[...].astype(F32)).astype(BF16)
    across = ((1,), (1,))
    flat = coeffs_ref[...].reshape(stored.shape[::-1])
    stored[...] = flat.astype(F32).T.astype(BF16)

    for copy in first:
        copy.wait_recv()
    halves = []
    for h in range(chans):
        held = rbuf[h].reshape(blocks, LANES)
        wide, even, odd = (dot(analysis[:, v * blocks:(v + 1) * blocks], held) for v in range(3))
        halves += [wide, even[:, :half] + odd[:, half:]]
    coef = jnp.concatenate(halves, axis=1).astype(BF16)

    part = w1s.shape[1]

    def weight(q):
        return dot(stored[pl.ds(pl.multiple_of(q * part, part), part), :], coef)

    reduce1 = []
    for p in range(quads - 1, 0, -1):
        q, px, pc = quad_peer(p)
        w1s[q] = weight(q).astype(BF16)
        copy = remote(w1s.at[q], w1r.at[p - 1], pair(r1sem, p - 1), {"ens": px, "chan": pc})
        copy.start()
        reduce1.append(copy)
    started += reduce1
    own = weight(quad)

    for h in range(chans):
        mixed = dot(coef, mix_ref[h * cols:(h + 1) * cols, :], across)
        rest = mixed[:, LANES:]
        none = jnp.zeros_like(rest)
        sides = (
            mixed[:, :LANES],
            jnp.concatenate([rest, none], axis=1),
            jnp.concatenate([none, rest], axis=1),
        )
        returned = sum(
            dot(synthesis[v * blocks:(v + 1) * blocks], side.astype(BF16))
            for v, side in enumerate(sides)
        )
        sbuf2[h] = returned.astype(BF16).reshape(lats, pad, LANES)
    second = []
    for p in range(1, owners):
        q, pz, pc = owner_peer(p)
        copy = remote(sbuf2.at[pc, pz], rbuf2.at[me], pair(fsem, p - 1), {"lat": pz, "chan": pc})
        copy.start()
        second.append(copy)
    started += second
    rbuf2[me] = sbuf2[c, z]

    total = own
    for p, copy in zip(range(quads - 1, 0, -1), reduce1):
        copy.wait_recv()
        total = total + w1r[p - 1].astype(F32)
    total = total.reshape(w2own.shape)
    w2own[...] = total
    w2s[...] = total.astype(BF16)
    reduce2 = []
    for p in range(1, lats):
        pz = lax.rem(z + p, lats)
        copy = remote(w2s.at[pz], w2r.at[p - 1], pair(r2sem, p - 1), {"lat": pz})
        copy.start()
        reduce2.append(copy)
    started += reduce2

    for copy in second:
        copy.wait_recv()
    spatial = dot(inv_ref[...], rbuf2[...].reshape(owners * pad, LANES))
    pairs = spatial[points:].reshape(-1, 1, lon, LANES)
    rest = jnp.concatenate([pairs[..., :half], pairs[..., half:]], axis=1).reshape(points, half)
    spatial = jnp.concatenate([spatial[:points], rest], axis=1)
    out_ref[...] = (grad_ref[...].astype(F32) + spatial).astype(BF16)

    piece = w2own[z]
    for p, copy in enumerate(reduce2):
        copy.wait_recv()
        piece = piece + w2r[p].astype(F32)
    full_ref[quad, z] = piece.astype(BF16)
    gather1 = []
    for p in range(1, lats):
        pz = lax.rem(z + p, lats)
        copy = remote(full_ref.at[quad, z], full_ref.at[quad, z], pair(g1sem, p - 1), {"lat": pz})
        copy.start()
        gather1.append(copy)
    started += gather1
    gather2 = []
    for s in range(lats):
        if s > 0:
            gather1[s - 1].wait_recv()
        source = lax.rem(z + lats - s, lats)
        for p in range(1, quads):
            q, px, pc = quad_peer(p)
            block = full_ref.at[quad, source]
            copy = remote(block, block, pair(g2sem, p - 1, s), {"ens": px, "chan": pc})
            copy.start()
            gather2.append(copy)
    mean = 1.0 / (members * lon // 2)
    for p in range(quads):
        if p > 0:
            for s in range(lats):
                gather2[s * (quads - 1) + p - 1].wait_recv()
        block = lax.rem(quad + quads - p, quads)
        weight_ref[pl.ds(pl.multiple_of(block * part, part), part), :] = (
            full_ref[block].astype(F32).reshape(part, chans * cols) * mean
        )
    started += gather2
    for copy in started:
        copy.wait_send()


def store_kernel(result, weight, result_hbm, weight_hbm, sems):
    stores = [
        pltpu.make_async_copy(weight, weight_hbm, sems.at[0]),
        pltpu.make_async_copy(result, result_hbm, sems.at[1]),
    ]
    for store in stores:
        store.start()
    for store in stores:
        store.wait()


def stored_whole(result, weight):
    return pl.pallas_call(
        store_kernel,
        out_shape=tuple(jax.ShapeDtypeStruct(x.shape, x.dtype) for x in (result, weight)),
        in_specs=[pl.BlockSpec(memory_space=pl.ANY)] * 2,
        out_specs=(pl.BlockSpec(memory_space=pltpu.HBM),) * 2,
        scratch_shapes=[pltpu.SemaphoreType.DMA((2,))],
        compiler_params=pltpu.CompilerParams(vmem_limit_bytes=1 << 20),
    )(result, weight)


def fused(grad_out, pre_act, coeffs, legendre, mixing):
    rows, lon, cols = grad_out.shape[1:]
    lats, chans = lax.axis_size("lat"), lax.axis_size("chan")
    members = lax.axis_size("ens")
    modes, degrees, held = legendre.shape
    owners, quads, channels = lats * chans, members * chans, cols * chans
    pad = padded(rows, 2 * modes)
    part, piece = channels // quads, channels // quads // lats
    constants = tables(rows, lon, lats, chans, members, modes, degrees)
    dma = pltpu.SemaphoreType.DMA

    def kernel(*refs):
        fused_kernel(lats, chans, members, lon, *refs)

    operands = (
        grad_out.reshape(rows * lon, cols),
        pre_act.reshape(rows * lon, cols),
        coeffs.reshape(modes * degrees, 2, channels),
        legendre.transpose(0, 2, 1),
        mixing,
        *constants,
    )
    operands = tuple(pltpu.with_memory_space_constraint(x, pltpu.HBM) for x in operands)
    result, weight = pl.pallas_call(
        kernel,
        out_shape=(
            pltpu.VMEM((rows * lon, cols), BF16),
            pltpu.VMEM((channels, channels), F32),
        ),
        in_specs=[pl.BlockSpec(memory_space=pltpu.HBM)] * 13,
        out_specs=(pl.BlockSpec(memory_space=pltpu.VMEM),) * 2,
        scratch_shapes=[
            pltpu.VMEM((quads, lats, piece, channels), BF16),
            *[pltpu.VMEM(operand.shape, BF16) for operand in operands],
            pltpu.VMEM((channels, modes * degrees * 2), BF16),
            pltpu.VMEM((modes, held, degrees), BF16),
            pltpu.VMEM((owners, pad, LANES), BF16),
            pltpu.VMEM((chans, lats, pad, LANES), BF16),
            pltpu.VMEM((chans, lats, pad, LANES), BF16),
            pltpu.VMEM((owners, pad, LANES), BF16),
            pltpu.VMEM((quads, part, channels), BF16),
            pltpu.VMEM((quads - 1, part, channels), BF16),
            pltpu.VMEM((lats, piece, channels), F32),
            pltpu.VMEM((lats, piece, channels), BF16),
            pltpu.VMEM((lats - 1, piece, channels), BF16),
            dma((len(operands),)),
            dma((2, 1)),
            dma((2, owners - 1)),
            dma((2, owners - 1)),
            dma((2, quads - 1)),
            dma((2, lats - 1)),
            dma((2, lats - 1)),
            dma((2, quads - 1, lats)),
        ],
        compiler_params=pltpu.CompilerParams(
            collective_id=0, has_side_effects=True, vmem_limit_bytes=48 << 20
        ),
    )(*operands)
    result, weight = stored_whole(result, weight)
    return result.reshape(grad_out.shape), weight


def fits(mesh, rows, lon, channels):
    lats, chans, members = (mesh.shape[axis] for axis in ("lat", "chan", "ens"))
    return (
        members == 2 and lats * chans <= 8 and rows * lon <= 512
        and lon % 16 == 0 and rows % 2 == 0
        and channels // mesh.shape["chan"] == LANES + LANES // 2
        and channels % (members * chans * lats * 8) == 0
    )


def solution(mesh):
    placed = (
        P(("grp", "ens"), "lat", None, "chan"),
        P(("grp", "ens"), "lat", None, "chan"),
        P(("grp", "ens"), ("lat", "chan"), None, None, None),
        P(("lat", "chan"), None, "ens"),
        P(),
    )

    def local(grad_out, *rest):
        rows, lon, cols = grad_out.shape[1:]
        small = fits(mesh, rows, lon, cols * mesh.shape["chan"])
        return (fused if small else on_device)(grad_out, *rest)

    return jax.shard_map(
        local,
        mesh=mesh,
        in_specs=placed,
        out_specs=(P(("grp", "ens"), "lat", None, "chan"), P("grp", None)),
        check_vma=False,
    )
```

```python
import math

import jax
import jax.numpy as jnp
import numpy as np
from jax import lax
from jax.experimental import pallas as pl
from jax.experimental.pallas import tpu as pltpu
from jax.sharding import PartitionSpec as P


def fourier_table(lon_count, mode_count):
    longitude = jnp.arange(lon_count, dtype=jnp.int32)[:, None]
    wavenumber = jnp.arange(mode_count, dtype=jnp.int32)[None, :]
    product_index = longitude * wavenumber % lon_count
    angles = 2.0 * math.pi / lon_count * product_index.astype(jnp.float32)
    factor = math.sqrt(2.0 / lon_count)
    stacked = jnp.stack([jnp.cos(angles), -jnp.sin(angles)], axis=2) * factor
    return stacked.reshape(lon_count, 2 * mode_count).astype(jnp.bfloat16)


def silu_backward(cotangent, preact):
    values = preact.astype(jnp.float32)
    gate_value = jax.nn.sigmoid(values)
    return (
        cotangent.astype(jnp.float32) * gate_value * (1.0 + values * (1.0 - gate_value))
    ).astype(jnp.bfloat16)


def on_device(grad_out, pre_act, coeffs, legendre, mixing):
    lat_rows = grad_out.shape[1]
    lon_count = grad_out.shape[2]
    chan_cols = grad_out.shape[3]
    mode_count = lon_count // 2
    lat_devices = lax.axis_size("lat")
    chan_count = lax.axis_size("chan")
    members = lax.axis_size("ens")
    lat_count = lat_rows * lat_devices
    channels = chan_cols * chan_count
    mode_width = 2 * mode_count // (lat_devices * chan_count)
    local_modes = mode_width // 2
    fourier = fourier_table(lon_count, mode_count)
    scaled = silu_backward(grad_out[0], pre_act[0])
    spectral = jnp.einsum(
        "nk,anc->akc", fourier, scaled, preferred_element_type=jnp.float32
    ).astype(jnp.bfloat16)
    exchanged = lax.all_to_all(
        lax.all_to_all(spectral, "lat", split_axis=1, concat_axis=0, tiled=True),
        "chan",
        split_axis=1,
        concat_axis=2,
        tiled=True,
    )
    spectral_modes = exchanged.reshape(lat_count, local_modes, 2, channels)
    legendre_full = lax.all_gather(legendre, "ens", axis=2, tiled=True)
    coef_grad = jnp.einsum(
        "mla,amrc->mlrc", legendre_full, spectral_modes, preferred_element_type=jnp.float32
    ).astype(jnp.bfloat16)
    stored = coeffs[0].reshape(-1, channels)
    flat_grad = coef_grad.reshape(-1, channels)
    weight_grad = lax.dot_general(
        stored, flat_grad, (((0,), (0,)), ((), ())), preferred_element_type=jnp.float32
    )
    weight_grad = weight_grad * (1.0 / (members * mode_count))
    weight_grad = lax.psum(weight_grad, ("lat", "chan", "ens"))
    mixed_grad = lax.dot_general(
        coef_grad, mixing, (((3,), (1,)), ((), ())), preferred_element_type=jnp.float32
    ).astype(jnp.bfloat16)
    returned = jnp.einsum(
        "mla,mlrc->amrc", legendre_full, mixed_grad, preferred_element_type=jnp.float32
    ).astype(jnp.bfloat16)
    shaped = returned.reshape(lat_count, 1, mode_width, channels)
    received = lax.all_to_all(
        lax.all_to_all(shaped, "lat", split_axis=0, concat_axis=1, tiled=True),
        "chan",
        split_axis=3,
        concat_axis=2,
        tiled=True,
    )
    row_coeffs = received.reshape(lat_rows, 2 * mode_count, chan_cols)
    spatial = jnp.einsum("nk,akc->anc", fourier, row_coeffs, preferred_element_type=jnp.float32)
    result = (grad_out[0].astype(jnp.float32) + spatial).astype(jnp.bfloat16)
    return (result[None], weight_grad)

MESH = pl.DeviceIdType.MESH
BF16 = jnp.bfloat16
F32 = jnp.float32


def dot(a, b, dims=((1,), (0,))):
    return lax.dot_general(a, b, (dims, ((), ())), preferred_element_type=F32)


LANES = 128


def slots(rows, width):
    whole = [(a, a, k) for a in range(rows) for k in range(width)]
    paired = [(a, a + 1, k) for a in range(0, rows, 2) for k in range(width)]
    return whole, paired


def padded(rows, width):
    return -(-(rows + rows // 2) * width // 16) * 16


def tables(rows, lon, lats, chans, members, modes, degrees):
    width = 2 * modes * chans
    pad = padded(rows, width)
    n = np.arange(lon)[:, None]
    m = np.arange(lon // 2)[None, :]
    angles = np.float32(2.0 * math.pi / lon) * (n * m % lon).astype(np.float32)
    table = np.stack([np.cos(angles), -np.sin(angles)], axis=2).reshape(lon, lon)
    table = (table * np.float32(math.sqrt(2.0 / lon))).astype(np.float32)
    groups = rows + rows // 2
    inverse = np.zeros((groups, lon, lats, pad), np.float32)
    for g in range(groups):
        for d in range(lats):
            inverse[g, :, d, g * width:(g + 1) * width] = table[:, d * width:(d + 1) * width]
    inverse = inverse.reshape(groups * lon, lats * pad)
    whole, paired = slots(rows, width)
    held = rows * lats // members
    step = -(-held // 16) * 16
    lat_of = np.full((3, lats, pad), -1)
    key_of = np.full((lats, pad), -1)
    for z in range(lats):
        for i, (even, odd, k) in enumerate(whole + paired):
            key_of[z, i] = k
            kinds = ((0, even),) if i < len(whole) else ((1, even), (2, odd))
            for kind, lat in kinds:
                lat = z * rows + lat
                lat_of[kind, z, i] = lat // held * step + lat % held
    lat_of, key_of = lat_of.reshape(3, -1), key_of.reshape(-1)
    select = (lat_of[:, None, :] == np.arange(members * step)[None, :, None]).astype(np.float32)
    row = np.arange(chans * modes * degrees * 2)
    spread = (np.arange(chans * modes * degrees)[:, None] == row[None, :] // 2).astype(np.float32)
    row_key = row // (2 * degrees) * 2 + row % 2
    mask = (row_key[:, None] == key_of[None, :]).astype(np.float32)
    cast = lambda x: jnp.asarray(np.ascontiguousarray(x), BF16)
    return (
        cast(inverse.T), cast(inverse), cast(select), cast(select.transpose(0, 2, 1)),
        cast(spread), cast(mask), cast(mask.T),
    )


def swap_halves(x):
    return pltpu.roll(x, LANES // 2, 1)


def lower_half(x):
    return lax.broadcasted_iota(jnp.int32, x.shape, 1) < LANES // 2


def joined(wide, even, odd):
    first, second = wide[:, :LANES], wide[:, LANES:]
    low = lower_half(first)
    none = jnp.zeros_like(first)
    middle = jnp.where(low, even[:, :LANES], none)
    middle = middle + swap_halves(jnp.where(low, second, odd[:, :LANES]))
    last = jnp.where(low, none, odd[:, LANES:])
    last = last + swap_halves(jnp.where(low, even[:, LANES:], second))
    return jnp.concatenate([first, middle, last], axis=1).astype(BF16)


def fused_kernel(
    lats, chans, members, lon,
    grad_hbm, pre_hbm, coeffs_hbm, leg_hbm, mix_hbm,
    fwd_hbm, inv_hbm, sel_hbm, selt_hbm, spread_hbm, mask_hbm, maskt_hbm,
    out_ref, weight_ref,
    grad_ref, pre_ref, coeffs_ref, lbuf, mix_ref,
    fwd_ref, inv_ref, sel_ref, selt_ref, spread_ref, mask_ref, maskt_ref,
    terms, sbuf, rbuf, sbuf2, rbuf2, w1s, w1r, full_ref,
    isem, lsem, lrsem, csem, esem, ersem, ssem, r1sem, r1rsem, gsem, grsem, hsem, fsem, frsem,
):
    z, c, x = lax.axis_index("lat"), lax.axis_index("chan"), lax.axis_index("ens")
    pad, blocks = rbuf.shape[2], lats * rbuf.shape[2]
    half = lats // 2
    high = z // half
    other = lax.rem(x + 1, members)
    sibling = {"chan": 1 - c}
    mine = z * members + x
    piece = full_ref.shape[1]

    def remote(src, dst, send, recv, target):
        return pltpu.make_async_remote_copy(
            src_ref=src, dst_ref=dst, send_sem=send, recv_sem=recv,
            device_id=target, device_id_type=MESH,
        )

    def arrived(ref, sem):
        pltpu.make_async_copy(ref, ref, sem).wait()

    def load(source, target, index):
        return pltpu.make_async_copy(source, target, isem.at[index])

    far_first = [high * j + (1 - high) * (lats - 1 - j) for j in range(half)]
    far_first += [high * half + lax.rem(z + j, half) for j in range(1, half)]

    urgent = [load(pre_hbm, pre_ref, 0), load(grad_hbm, grad_ref, 1), load(fwd_hbm, fwd_ref, 2)]
    shared = [
        load(leg_hbm, lbuf.at[x, c], 3), load(spread_hbm, spread_ref, 4),
        load(sel_hbm, sel_ref, 5), load(mask_hbm, mask_ref, 6),
    ]
    late = load(inv_hbm, inv_ref, 7)
    own_coeffs = load(coeffs_hbm, coeffs_ref.at[1], 8)
    inner = [load(selt_hbm, selt_ref, 8), load(maskt_hbm, maskt_ref, 9), load(mix_hbm, mix_ref, 10)]
    for copy in urgent + shared:
        copy.start()

    barrier = pltpu.get_barrier_semaphore()
    for pz in far_first + [z]:
        for px in (other, x):
            for pc in (1 - c, c):
                if pz is z and px is x and pc is c:
                    continue
                pl.semaphore_signal(
                    barrier, inc=1, device_id={"lat": pz, "ens": px, "chan": pc},
                    device_id_type=MESH,
                )

    @pl.when(c == 0)
    def _():
        for copy in inner:
            copy.start()

    @pl.when(c == 1)
    def _():
        own_coeffs.start()

    late.start()

    for copy in urgent:
        copy.wait()
    values = pre_ref[...].astype(F32)
    gate = jax.nn.sigmoid(values)
    scaled = grad_ref[...].astype(F32) * gate * (1.0 + values * (1.0 - gate))
    points = scaled.shape[0]
    tail = scaled[:, LANES:].reshape(-1, 2, lon, LANES // 2)
    paired = jnp.concatenate([tail[:, 0], tail[:, 1]], axis=-1).reshape(-1, LANES)
    packed = jnp.concatenate([scaled[:, :LANES], paired], axis=0).astype(BF16)
    sbuf[...] = dot(fwd_ref[...], packed).astype(BF16).reshape(lats, pad, LANES)

    pl.semaphore_wait(barrier, lats * members * chans - 1)

    first = [
        remote(sbuf.at[q], rbuf.at[c, z], esem.at[q], ersem.at[c, z], {"lat": q, "chan": 1})
        for q in far_first
    ]
    for copy in first:
        copy.start()
    legs = [
        remote(leg_hbm, lbuf.at[x, c], lsem.at[i], lrsem.at[x, c], {"ens": px, "chan": pc})
        for i, (px, pc) in enumerate(((other, c), (other, 1 - c), (x, 1 - c)))
    ]
    for copy in legs:
        copy.start()

    def transforms():
        for copy in shared:
            copy.wait()
        for px, pc in ((x, 1 - c), (other, 1 - c), (other, c)):
            arrived(lbuf.at[px, pc], lrsem.at[px, pc])
        modes, held, degrees = lbuf.shape[2:]
        fill = sel_ref.shape[1] // members - held
        parts = []
        for px in range(members):
            row = [lbuf[px, pc, m].astype(F32) for pc in range(chans) for m in range(modes)]
            parts.append(jnp.concatenate(row, axis=1))
            parts.append(jnp.zeros((fill, parts[0].shape[1]), F32))
        maps = jnp.concatenate(parts, axis=0).astype(BF16)
        maps = dot(maps, spread_ref[...]).astype(BF16)
        down = ((0,), (0,))
        analysis = [dot(maps, sel_ref[v], down).astype(BF16) * mask_ref[...] for v in range(3)]
        return maps, analysis

    def received():
        return jnp.concatenate([rbuf[h].reshape(blocks, LANES) for h in range(chans)], axis=1)

    def back_to_grid():
        late.wait()
        spatial = dot(inv_ref[...], rbuf2[...].reshape(blocks, LANES))
        pairs = spatial[points:].reshape(-1, 1, lon, LANES)
        low, up = pairs[..., :LANES // 2], pairs[..., LANES // 2:]
        rest = jnp.concatenate([low, up], axis=1).reshape(points, LANES // 2)
        spatial = jnp.concatenate([spatial[:points], rest], axis=1)
        out_ref[...] = (grad_ref[...].astype(F32) + spatial).astype(BF16)

    mean = 1.0 / (members * lon // 2)

    def average(index):
        rows = pl.ds(pl.multiple_of(index * piece, piece), piece)
        weight_ref[rows, :] = full_ref[index].astype(F32) * mean

    near_first = [z] + far_first[::-1]
    order = [(pz, px) for pz in near_first for px in (x, other)][1:]

    @pl.when(c == 0)
    def _():
        block = remote(sbuf.at[z], rbuf.at[c, z], esem.at[z], ersem.at[c, z], sibling)
        block.start()
        passed = remote(coeffs_hbm, coeffs_ref.at[0], csem.at[0], csem.at[1], sibling)
        passed.start()
        maps, analysis = transforms()
        for copy in inner:
            copy.wait()
        synthesis = [dot(selt_ref[v], maps).astype(BF16) * maskt_ref[...] for v in range(3)]

        arrived(rbuf, ssem.at[1])
        held = received()
        coef = joined(*(dot(matrix, held) for matrix in analysis))
        mixed = dot(coef, mix_ref[...], ((1,), (1,)))
        t0, t1, t2 = (mixed[:, i * LANES:(i + 1) * LANES] for i in range(3))
        low = lower_half(t0)
        none = jnp.zeros_like(t0)
        even0, odd1 = jnp.where(low, t1, none), jnp.where(low, none, t2)
        sides = (
            (t0, swap_halves(jnp.where(low, t2, t1))),
            (even0, swap_halves(odd1)),
            (swap_halves(even0), odd1),
        )
        back = sum(
            dot(matrix, jnp.concatenate(side, axis=1).astype(BF16))
            for matrix, side in zip(synthesis, sides)
        ).astype(BF16)
        for h in range(chans):
            sbuf2[h] = back[:, h * LANES:(h + 1) * LANES].reshape(lats, pad, LANES)
        second = [
            remote(
                sbuf2.at[h, q], rbuf2.at[z], fsem.at[h, q], frsem.at[z], {"lat": q, "chan": h}
            )
            for q in far_first for h in range(chans)
        ]
        second.append(remote(sbuf2.at[1, z], rbuf2.at[z], fsem.at[1, z], frsem.at[z], sibling))
        for copy in second:
            copy.start()
        rbuf2[z] = sbuf2[0, z]
        for q in far_first[::-1]:
            arrived(rbuf2.at[q], frsem.at[q])
        back_to_grid()
        for pz, px in [(z, x)] + order:
            index = pz * members + px
            arrived(full_ref.at[index], grsem.at[index])
            average(index)
        for copy in second + [block, passed]:
            copy.wait_send()

    @pl.when(c == 1)
    def _():
        rbuf[1, z] = sbuf[z]
        _, analysis = transforms()
        own_coeffs.wait()
        arrived(coeffs_ref.at[0], csem.at[1])
        flat = coeffs_ref[...].reshape(-1, coeffs_ref.shape[-1])
        stored = flat.astype(F32).T.astype(BF16)
        for v in range(3):
            terms[:, v] = dot(stored, analysis[v]).astype(BF16).reshape(2, -1, blocks)

        arrived(rbuf.at[0, z], ersem.at[0, z])
        for q in far_first[::-1]:
            for h in range(chans):
                arrived(rbuf.at[h, q], ersem.at[h, q])
        block = remote(rbuf, rbuf, ssem.at[0], ssem.at[1], sibling)
        block.start()
        held = received()
        reduce = []
        for group, targets in ((1 - high, far_first[:half]), (high, far_first[half:] + [z])):
            value = joined(*(dot(terms[group, v], held) for v in range(3)))
            count = half * members
            rows = pl.ds(group * count, count)
            w1s[rows] = value.reshape(count, piece, value.shape[1])
            for pz in targets:
                for px in (other, x):
                    if pz is z and px is x:
                        continue
                    q = pz * members + px
                    copy = remote(
                        w1s.at[q], w1r.at[mine], r1sem.at[q], r1rsem.at[mine],
                        {"lat": pz, "ens": px},
                    )
                    copy.start()
                    reduce.append(copy)
        w1r[mine] = w1s[mine]
        for pz, px in order:
            q = pz * members + px
            arrived(w1r.at[q], r1rsem.at[q])
        total = w1r[0].astype(F32)
        for q in range(1, lats * members):
            total = total + w1r[q].astype(F32)
        full_ref[mine] = total.astype(BF16)
        gather = []
        for pz in far_first + [z]:
            for px in (other, x):
                if pz is z and px is x:
                    continue
                q = pz * members + px
                copy = remote(
                    full_ref.at[mine], full_ref.at[mine], gsem.at[q], grsem.at[mine],
                    {"lat": pz, "ens": px},
                )
                copy.start()
                gather.append(copy)
        forward = []
        for pz, px in [(z, x)] + order:
            index = pz * members + px
            if not (pz is z and px is x):
                arrived(full_ref.at[index], grsem.at[index])
            copy = remote(
                full_ref.at[index], full_ref.at[index], hsem.at[index], grsem.at[index], sibling
            )
            copy.start()
            forward.append(copy)
            average(index)
        for q in [z] + far_first[::-1]:
            arrived(rbuf2.at[q], frsem.at[q])
        back_to_grid()
        for copy in [block] + reduce + gather + forward:
            copy.wait_send()

    for copy in first + legs:
        copy.wait_send()


def store_kernel(result, weight, result_hbm, weight_hbm, sems):
    stores = [
        pltpu.make_async_copy(weight, weight_hbm, sems.at[0]),
        pltpu.make_async_copy(result, result_hbm, sems.at[1]),
    ]
    for store in stores:
        store.start()
    for store in stores:
        store.wait()


def stored_whole(result, weight):
    return pl.pallas_call(
        store_kernel,
        out_shape=tuple(jax.ShapeDtypeStruct(x.shape, x.dtype) for x in (result, weight)),
        in_specs=[pl.BlockSpec(memory_space=pl.ANY)] * 2,
        out_specs=(pl.BlockSpec(memory_space=pltpu.HBM),) * 2,
        scratch_shapes=[pltpu.SemaphoreType.DMA((2,))],
        compiler_params=pltpu.CompilerParams(vmem_limit_bytes=1 << 20),
    )(result, weight)


def fused(grad_out, pre_act, coeffs, legendre, mixing):
    rows, lon, cols = grad_out.shape[1:]
    lats, chans = lax.axis_size("lat"), lax.axis_size("chan")
    members = lax.axis_size("ens")
    modes, degrees, held = legendre.shape
    channels = cols * chans
    pad = padded(rows, 2 * modes * chans)
    pieces = lats * members
    piece = channels // pieces
    constants = tables(rows, lon, lats, chans, members, modes, degrees)
    dma = pltpu.SemaphoreType.DMA

    def kernel(*refs):
        fused_kernel(lats, chans, members, lon, *refs)

    operands = (
        grad_out.reshape(rows * lon, cols),
        pre_act.reshape(rows * lon, cols),
        coeffs.reshape(modes * degrees, 2, channels),
        legendre.transpose(0, 2, 1),
        mixing,
        *constants,
    )
    operands = tuple(pltpu.with_memory_space_constraint(x, pltpu.HBM) for x in operands)
    result, weight = pl.pallas_call(
        kernel,
        out_shape=(
            pltpu.VMEM((rows * lon, cols), BF16),
            pltpu.VMEM((channels, channels), F32),
        ),
        in_specs=[pl.BlockSpec(memory_space=pltpu.HBM)] * len(operands),
        out_specs=(pl.BlockSpec(memory_space=pltpu.VMEM),) * 2,
        scratch_shapes=[
            pltpu.VMEM((rows * lon, cols), BF16),
            pltpu.VMEM((rows * lon, cols), BF16),
            pltpu.VMEM((chans, modes * degrees, 2, channels), BF16),
            pltpu.VMEM((members, chans, modes, held, degrees), BF16),
            pltpu.VMEM(mixing.shape, BF16),
            *[pltpu.VMEM(constant.shape, BF16) for constant in constants],
            pltpu.VMEM((2, 3, channels // 2, lats * pad), BF16),
            pltpu.VMEM((lats, pad, LANES), BF16),
            pltpu.VMEM((chans, lats, pad, LANES), BF16),
            pltpu.VMEM((chans, lats, pad, LANES), BF16),
            pltpu.VMEM((lats, pad, LANES), BF16),
            pltpu.VMEM((pieces, piece, channels), BF16),
            pltpu.VMEM((pieces, piece, channels), BF16),
            pltpu.VMEM((pieces, piece, channels), BF16),
            dma((11,)),
            dma((members * chans - 1,)),
            dma((members, chans)),
            dma((2,)),
            dma((lats,)),
            dma((chans, lats)),
            dma((2,)),
            dma((pieces,)),
            dma((pieces,)),
            dma((pieces,)),
            dma((pieces,)),
            dma((pieces,)),
            dma((chans, lats)),
            dma((lats,)),
        ],
        compiler_params=pltpu.CompilerParams(
            collective_id=0, has_side_effects=True, vmem_limit_bytes=48 << 20
        ),
    )(*operands)
    result, weight = stored_whole(result, weight)
    return result.reshape(grad_out.shape), weight


def fits(mesh, rows, lon, channels):
    lats, chans, members = (mesh.shape[axis] for axis in ("lat", "chan", "ens"))
    return (
        members == 2 and chans == 2 and lats % 2 == 0 and lats <= 4 and rows * lon <= 512
        and lon % 16 == 0 and rows % 2 == 0
        and channels // chans == LANES + LANES // 2
        and channels % (members * lats * 16) == 0
    )


def solution(mesh):
    placed = (
        P(("grp", "ens"), "lat", None, "chan"),
        P(("grp", "ens"), "lat", None, "chan"),
        P(("grp", "ens"), ("lat", "chan"), None, None, None),
        P(("lat", "chan"), None, "ens"),
        P(),
    )

    def local(grad_out, *rest):
        rows, lon, cols = grad_out.shape[1:]
        small = fits(mesh, rows, lon, cols * mesh.shape["chan"])
        return (fused if small else on_device)(grad_out, *rest)

    return jax.shard_map(
        local,
        mesh=mesh,
        in_specs=placed,
        out_specs=(P(("grp", "ens"), "lat", None, "chan"), P("grp", None)),
        check_vma=False,
    )
```

```python
import math

import jax
import jax.numpy as jnp
import numpy as np
from jax import lax
from jax.experimental import pallas as pl
from jax.experimental.pallas import tpu as pltpu
from jax.sharding import PartitionSpec as P


def fourier_table(lon_count, mode_count):
    longitude = jnp.arange(lon_count, dtype=jnp.int32)[:, None]
    wavenumber = jnp.arange(mode_count, dtype=jnp.int32)[None, :]
    product_index = longitude * wavenumber % lon_count
    angles = 2.0 * math.pi / lon_count * product_index.astype(jnp.float32)
    factor = math.sqrt(2.0 / lon_count)
    stacked = jnp.stack([jnp.cos(angles), -jnp.sin(angles)], axis=2) * factor
    return stacked.reshape(lon_count, 2 * mode_count).astype(jnp.bfloat16)


def silu_backward(cotangent, preact):
    values = preact.astype(jnp.float32)
    gate_value = jax.nn.sigmoid(values)
    return (
        cotangent.astype(jnp.float32) * gate_value * (1.0 + values * (1.0 - gate_value))
    ).astype(jnp.bfloat16)


def on_device(grad_out, pre_act, coeffs, legendre, mixing):
    lat_rows = grad_out.shape[1]
    lon_count = grad_out.shape[2]
    chan_cols = grad_out.shape[3]
    mode_count = lon_count // 2
    lat_devices = lax.axis_size("lat")
    chan_count = lax.axis_size("chan")
    members = lax.axis_size("ens")
    lat_count = lat_rows * lat_devices
    channels = chan_cols * chan_count
    mode_width = 2 * mode_count // (lat_devices * chan_count)
    local_modes = mode_width // 2
    fourier = fourier_table(lon_count, mode_count)
    scaled = silu_backward(grad_out[0], pre_act[0])
    spectral = jnp.einsum(
        "nk,anc->akc", fourier, scaled, preferred_element_type=jnp.float32
    ).astype(jnp.bfloat16)
    exchanged = lax.all_to_all(
        lax.all_to_all(spectral, "lat", split_axis=1, concat_axis=0, tiled=True),
        "chan",
        split_axis=1,
        concat_axis=2,
        tiled=True,
    )
    spectral_modes = exchanged.reshape(lat_count, local_modes, 2, channels)
    legendre_full = lax.all_gather(legendre, "ens", axis=2, tiled=True)
    coef_grad = jnp.einsum(
        "mla,amrc->mlrc", legendre_full, spectral_modes, preferred_element_type=jnp.float32
    ).astype(jnp.bfloat16)
    stored = coeffs[0].reshape(-1, channels)
    flat_grad = coef_grad.reshape(-1, channels)
    weight_grad = lax.dot_general(
        stored, flat_grad, (((0,), (0,)), ((), ())), preferred_element_type=jnp.float32
    )
    weight_grad = weight_grad * (1.0 / (members * mode_count))
    weight_grad = lax.psum(weight_grad, ("lat", "chan", "ens"))
    mixed_grad = lax.dot_general(
        coef_grad, mixing, (((3,), (1,)), ((), ())), preferred_element_type=jnp.float32
    ).astype(jnp.bfloat16)
    returned = jnp.einsum(
        "mla,mlrc->amrc", legendre_full, mixed_grad, preferred_element_type=jnp.float32
    ).astype(jnp.bfloat16)
    shaped = returned.reshape(lat_count, 1, mode_width, channels)
    received = lax.all_to_all(
        lax.all_to_all(shaped, "lat", split_axis=0, concat_axis=1, tiled=True),
        "chan",
        split_axis=3,
        concat_axis=2,
        tiled=True,
    )
    row_coeffs = received.reshape(lat_rows, 2 * mode_count, chan_cols)
    spatial = jnp.einsum("nk,akc->anc", fourier, row_coeffs, preferred_element_type=jnp.float32)
    result = (grad_out[0].astype(jnp.float32) + spatial).astype(jnp.bfloat16)
    return (result[None], weight_grad)

MESH = pl.DeviceIdType.MESH
BF16 = jnp.bfloat16
F32 = jnp.float32


def dot(a, b, dims=((1,), (0,))):
    return lax.dot_general(a, b, (dims, ((), ())), preferred_element_type=F32)


LANES = 128


def slots(rows, width):
    whole = [(a, a, k) for a in range(rows) for k in range(width)]
    paired = [(a, a + 1, k) for a in range(0, rows, 2) for k in range(width)]
    return whole, paired


def padded(rows, width):
    return -(-(rows + rows // 2) * width // 16) * 16


def tables(rows, lon, lats, chans, members, modes, degrees):
    width = 2 * modes * chans
    pad = padded(rows, width)
    n = np.arange(lon)[:, None]
    m = np.arange(lon // 2)[None, :]
    angles = np.float32(2.0 * math.pi / lon) * (n * m % lon).astype(np.float32)
    table = np.stack([np.cos(angles), -np.sin(angles)], axis=2).reshape(lon, lon)
    table = (table * np.float32(math.sqrt(2.0 / lon))).astype(np.float32)
    groups = rows + rows // 2
    inverse = np.zeros((groups, lon, lats, pad), np.float32)
    for g in range(groups):
        for d in range(lats):
            inverse[g, :, d, g * width:(g + 1) * width] = table[:, d * width:(d + 1) * width]
    inverse = inverse.reshape(groups * lon, lats * pad)
    whole, paired = slots(rows, width)
    near = lats // members
    lat_of = np.full((3, near, pad), -1)
    key_of = np.full((near, pad), -1)
    for z in range(near):
        for i, (even, odd, k) in enumerate(whole + paired):
            key_of[z, i] = k
            kinds = ((0, even),) if i < len(whole) else ((1, even), (2, odd))
            for kind, lat in kinds:
                lat_of[kind, z, i] = z * rows + lat
    lat_of, key_of = lat_of.reshape(3, -1), key_of.reshape(-1)
    select = (lat_of[:, None, :] == np.arange(near * rows)[None, :, None]).astype(np.float32)
    row = np.arange(chans * modes * degrees * 2)
    spread = (np.arange(chans * modes * degrees)[:, None] == row[None, :] // 2).astype(np.float32)
    row_key = row // (2 * degrees) * 2 + row % 2
    mask = (row_key[:, None] == key_of[None, :]).astype(np.float32)
    width = lats * pad
    tables = [mask, mask.T, spread]
    tables += [np.pad(part, ((0, -part.shape[0] % 16), (0, 0))) for part in select]
    tables = [np.pad(part, ((0, 0), (0, width - part.shape[1]))) for part in tables + [inverse]]
    starts = np.cumsum([0] + [part.shape[0] for part in tables]).tolist()
    cast = lambda x: jnp.asarray(np.ascontiguousarray(x), BF16)
    return cast(inverse.T), cast(np.concatenate(tables, axis=0)), starts


def swap_halves(x):
    return pltpu.roll(x, LANES // 2, 1)


def lower_half(x):
    return lax.broadcasted_iota(jnp.int32, x.shape, 1) < LANES // 2


def joined(wide, even, odd):
    first, second = wide[:, :LANES], wide[:, LANES:]
    low = lower_half(first)
    none = jnp.zeros_like(first)
    middle = jnp.where(low, even[:, :LANES], none)
    middle = middle + swap_halves(jnp.where(low, second, odd[:, :LANES]))
    last = jnp.where(low, none, odd[:, LANES:])
    last = last + swap_halves(jnp.where(low, even[:, LANES:], second))
    return jnp.concatenate([first, middle, last], axis=1).astype(BF16)


def fused_kernel(
    lats, chans, members, lon, starts,
    grad_hbm, pre_hbm, coeffs_hbm, leg_hbm, mix_hbm, fwd_hbm, table_hbm,
    out_ref, weight_ref,
    point_ref, coeffs_ref, lbuf, mix_ref, fwd_ref, table_ref,
    terms, sbuf, rbuf, sbuf2, rbuf2, w1s, w1r, full_ref,
    isem, lsem, esem, ssem, rsem, gsem,
):
    z, c, x = lax.axis_index("lat"), lax.axis_index("chan"), lax.axis_index("ens")
    pad = rbuf.shape[1]
    half = lats // 2
    high = z // half
    other = lax.rem(x + 1, members)
    sibling = {"chan": 1 - c}
    mine = z * members + x
    pieces, piece = full_ref.shape[:2]
    modes, held, degrees = lbuf.shape[1:]
    points = point_ref.shape[1]
    count, near = 2 * chans * modes * degrees, half * pad
    early_first = sorted(
        ((a, b) for a in range(lats) for b in range(members)), key=lambda place: (sum(place), place)
    )

    def table(index, rows, cols):
        return table_ref[starts[index]:starts[index] + rows, :cols]

    def remote(src, dst, send, recv, target):
        return pltpu.make_async_remote_copy(
            src_ref=src, dst_ref=dst, send_sem=send, recv_sem=recv,
            device_id=target, device_id_type=MESH,
        )

    def done(ref, sem):
        pltpu.make_async_copy(ref, ref, sem).wait()

    far_first = [high * j + (1 - high) * (lats - 1 - j) for j in range(half)]
    far_first += [high * half + lax.rem(z + j, half) for j in range(1, half)]
    near_first = [z] + far_first[::-1]
    order = [(pz, px) for pz in near_first for px in (x, other)][1:]

    def load(source, target, index):
        return pltpu.make_async_copy(source, target, isem.at[index])

    urgent = load(fwd_hbm, fwd_ref, 1)
    shared = [load(leg_hbm, lbuf.at[x * chans + c], 2), load(table_hbm, table_ref, 3)]
    own_coeffs = load(coeffs_hbm, coeffs_ref.at[1], 4)
    own_mix = load(mix_hbm, mix_ref, 4)
    load(pre_hbm, point_ref.at[0], 0).start()
    load(grad_hbm, point_ref.at[1], 0).start()
    urgent.start()

    barrier = pltpu.get_barrier_semaphore()

    def announce(**target):
        pl.semaphore_signal(barrier, inc=1, device_id=target, device_id_type=MESH)

    @pl.when(c == 1)
    def _():
        for pz in far_first:
            for pc in (0, 1):
                announce(lat=pz, chan=pc)

    announce(ens=other, chan=c)
    announce(ens=other, chan=1 - c)
    announce(chan=1 - c)

    for copy in shared:
        copy.start()

    @pl.when(c == 0)
    def _():
        own_mix.start()

    @pl.when(c == 1)
    def _():
        own_coeffs.start()

    done(point_ref, isem.at[0])
    urgent.wait()
    values = point_ref[0].astype(F32)
    gate = jax.nn.sigmoid(values)
    scaled = point_ref[1].astype(F32) * gate * (1.0 + values * (1.0 - gate))
    tail = scaled[:, LANES:].reshape(-1, 2, lon, LANES // 2)
    paired = jnp.concatenate([tail[:, 0], tail[:, 1]], axis=-1).reshape(-1, LANES)
    packed = jnp.concatenate([scaled[:, :LANES], paired], axis=0).astype(BF16)
    sbuf[...] = dot(fwd_ref[...], packed).astype(BF16).reshape(lats, pad, LANES)

    pl.semaphore_wait(barrier, lats + members * chans - 2)

    leg = x * chans + c
    for px, pc, kind in ((other, c, 1), (other, 1 - c, 1), (x, 1 - c, 0)):
        remote(
            leg_hbm, lbuf.at[leg], lsem.at[0], lsem.at[1 + kind], {"ens": px, "chan": pc}
        ).start()
    for q in far_first:
        remote(
            sbuf.at[q], rbuf.at[c * lats + z], esem.at[0], esem.at[1], {"lat": q, "chan": 1}
        ).start()

    def transform(px):
        row = [lbuf[px * chans + pc, m].astype(F32) for pc in range(chans) for m in range(modes)]
        spread = table(2, count // 2, count)
        maps = dot(jnp.concatenate(row, axis=1).astype(BF16), spread).astype(BF16)
        down = ((0,), (0,))
        analysis = [
            dot(maps, table(3 + v, held, near), down).astype(BF16) * table(0, count, near)
            for v in range(3)
        ]
        return maps, analysis

    def maps_here():
        for copy in shared:
            copy.wait()
        done(lbuf.at[x * chans + 1 - c], lsem.at[1])

    def maps_there():
        done(lbuf.at[pl.ds(other * chans, chans)], lsem.at[2])

    def received(px):
        return jnp.concatenate(
            [rbuf[pl.ds(h * lats + px * half, half)].reshape(-1, LANES) for h in range(chans)],
            axis=1,
        )

    def back_to_grid():
        inverse = table(6, points + points // 2, lats * pad)
        spatial = dot(inverse, rbuf2[...].reshape(lats * pad, LANES))
        pairs = spatial[points:].reshape(-1, 1, lon, LANES)
        low, up = pairs[..., :LANES // 2], pairs[..., LANES // 2:]
        rest = jnp.concatenate([low, up], axis=1).reshape(points, LANES // 2)
        spatial = jnp.concatenate([spatial[:points], rest], axis=1)
        out_ref[...] = (point_ref[1].astype(F32) + spatial).astype(BF16)

    mean = 1.0 / (members * lon // 2)

    def average(pz):
        start = pz * members * piece
        rows = pl.ds(pl.multiple_of(start, members * piece), members * piece)
        value = full_ref[pl.ds(pz * members, members)].astype(F32) * mean
        weight_ref[rows, :] = value.reshape(members * piece, value.shape[2])

    @pl.when(c == 0)
    def _():
        passed = remote(coeffs_hbm, coeffs_ref.at[0], ssem.at[0], ssem.at[1], sibling)
        passed.start()
        remote(
            sbuf.at[z], rbuf.at[c * lats + z], esem.at[0], esem.at[1], sibling
        ).start()
        maps_here()
        near_maps, near_down = transform(x)
        own_mix.wait()

        def upward(maps):
            down = ((0,), (0,))
            return [
                dot(table(3 + v, held, near), maps, down).astype(BF16) * table(1, near, count)
                for v in range(3)
            ]

        near_up = upward(near_maps)
        maps_there()
        far_maps, far_down = transform(other)
        far_up = upward(far_maps)
        done(rbuf, ssem.at[1])
        block = received(x), received(other)
        coef = joined(*(dot(near_down[v], block[0]) + dot(far_down[v], block[1]) for v in range(3)))
        mixed = dot(coef, mix_ref[...], ((1,), (1,)))
        t0, t1, t2 = (mixed[:, i * LANES:(i + 1) * LANES] for i in range(3))
        low = lower_half(t0)
        none = jnp.zeros_like(t0)
        even0, odd1 = jnp.where(low, t1, none), jnp.where(low, none, t2)
        sides = (
            (t0, swap_halves(jnp.where(low, t2, t1))),
            (even0, swap_halves(odd1)),
            (swap_halves(even0), odd1),
        )
        sides = [jnp.concatenate(side, axis=1).astype(BF16) for side in sides]
        for px, synthesis in ((other, far_up), (x, near_up)):
            back = sum(dot(matrix, side) for matrix, side in zip(synthesis, sides)).astype(BF16)
            for h in range(chans):
                part = back[:, h * LANES:(h + 1) * LANES].reshape(half, pad, LANES)
                sbuf2[pl.ds(h * lats + px * half, half)] = part
        for q in far_first:
            for h in range(chans):
                remote(
                    sbuf2.at[h * lats + q], rbuf2.at[z], rsem.at[0], rsem.at[2],
                    {"lat": q, "chan": h},
                ).start()
        remote(sbuf2.at[lats + z], rbuf2.at[z], rsem.at[0], rsem.at[2], sibling).start()
        rbuf2[z] = sbuf2[z]
        done(rbuf2.at[pl.ds(0, lats - 1)], rsem.at[2])
        back_to_grid()
        for pz in near_first:
            done(full_ref.at[pl.ds(pz * members, members)], gsem.at[2 + pz])
            average(pz)
        passed.wait_send()
        done(sbuf, esem.at[0])
        done(sbuf2.at[pl.ds(0, chans * lats - 1)], rsem.at[0])

    @pl.when(c == 1)
    def _():
        rbuf[lats + z] = sbuf[z]
        own_coeffs.wait()
        done(coeffs_ref.at[0], ssem.at[1])
        flat = coeffs_ref[...].reshape(-1, coeffs_ref.shape[-1])
        stored = flat.astype(F32).T.astype(BF16)
        maps_here()
        for px in (x, other):
            if px is other:
                maps_there()
            _, analysis = transform(px)
            for v in range(3):
                value = dot(stored, analysis[v]).astype(BF16)
                terms[px, :, v] = value.reshape(2, -1, value.shape[1])

        done(rbuf.at[pl.ds(0, chans * lats - 1)], esem.at[1])
        block = remote(rbuf, rbuf, ssem.at[0], ssem.at[1], sibling)
        block.start()
        arrays = received(0), received(1)
        for group, targets in ((1 - high, far_first[:half]), (high, far_first[half:] + [z])):
            value = joined(*(
                dot(terms[0, group, v], arrays[0]) + dot(terms[1, group, v], arrays[1])
                for v in range(3)
            ))
            share = half * members
            w1s[pl.ds(group * share, share)] = value.reshape(share, piece, value.shape[1])
            for pz in targets:
                for px in (other, x):
                    if pz is z and px is x:
                        continue
                    remote(
                        w1s.at[pz * members + px], w1r.at[mine], rsem.at[0], rsem.at[1],
                        {"lat": pz, "ens": px},
                    ).start()
        done(w1r.at[pl.ds(0, pieces - 1)], rsem.at[1])
        total = w1s[mine].astype(F32)
        for pz, px in order:
            total = total + w1r[pz * members + px].astype(F32)
        full_ref[mine] = total.astype(BF16)
        for pz, px in early_first:
            copy = remote(
                full_ref.at[mine], full_ref.at[mine], gsem.at[0], gsem.at[2 + z],
                {"lat": pz, "ens": px},
            )
            pl.when(jnp.logical_or(z != pz, x != px))(copy.start)
        for pz in near_first:
            both = full_ref.at[pl.ds(pz * members, members)]
            done(full_ref.at[z * members + other] if pz is z else both, gsem.at[2 + pz])
            remote(both, both, gsem.at[1], gsem.at[2 + pz], sibling).start()
            average(pz)
        done(rbuf2, rsem.at[2])
        back_to_grid()
        block.wait_send()
        done(sbuf.at[pl.ds(0, lats - 1)], esem.at[0])
        done(w1s.at[pl.ds(0, pieces - 1)], rsem.at[0])
        done(full_ref.at[pl.ds(0, pieces - 1)], gsem.at[0])
        done(full_ref, gsem.at[1])

    done(lbuf.at[pl.ds(0, members * chans - 1)], lsem.at[0])


def store_kernel(result, weight, result_hbm, weight_hbm, sems):
    stores = [
        pltpu.make_async_copy(weight, weight_hbm, sems.at[0]),
        pltpu.make_async_copy(result, result_hbm, sems.at[1]),
    ]
    for store in stores:
        store.start()
    for store in stores:
        store.wait()


def stored_whole(result, weight):
    return pl.pallas_call(
        store_kernel,
        out_shape=tuple(jax.ShapeDtypeStruct(x.shape, x.dtype) for x in (result, weight)),
        in_specs=[pl.BlockSpec(memory_space=pl.ANY)] * 2,
        out_specs=(pl.BlockSpec(memory_space=pltpu.HBM),) * 2,
        scratch_shapes=[pltpu.SemaphoreType.DMA((2,))],
        compiler_params=pltpu.CompilerParams(vmem_limit_bytes=1 << 20),
    )(result, weight)


def fused(grad_out, pre_act, coeffs, legendre, mixing):
    rows, lon, cols = grad_out.shape[1:]
    lats, chans = lax.axis_size("lat"), lax.axis_size("chan")
    members = lax.axis_size("ens")
    modes, degrees, held = legendre.shape
    channels = cols * chans
    pad = padded(rows, 2 * modes * chans)
    pieces = lats * members
    piece = channels // pieces
    *constants, starts = tables(rows, lon, lats, chans, members, modes, degrees)
    dma = pltpu.SemaphoreType.DMA

    def kernel(*refs):
        fused_kernel(lats, chans, members, lon, starts, *refs)

    operands = (
        grad_out.reshape(rows * lon, cols),
        pre_act.reshape(rows * lon, cols),
        coeffs.reshape(modes * degrees, 2, channels),
        legendre.transpose(0, 2, 1),
        mixing,
        *constants,
    )
    operands = tuple(pltpu.with_memory_space_constraint(x, pltpu.HBM) for x in operands)
    result, weight = pl.pallas_call(
        kernel,
        out_shape=(
            pltpu.VMEM((rows * lon, cols), BF16),
            pltpu.VMEM((channels, channels), F32),
        ),
        in_specs=[pl.BlockSpec(memory_space=pltpu.HBM)] * len(operands),
        out_specs=(pl.BlockSpec(memory_space=pltpu.VMEM),) * 2,
        scratch_shapes=[
            pltpu.VMEM((2, rows * lon, cols), BF16),
            pltpu.VMEM((chans, modes * degrees, 2, channels), BF16),
            pltpu.VMEM((members * chans, modes, held, degrees), BF16),
            pltpu.VMEM(mixing.shape, BF16),
            *[pltpu.VMEM(constant.shape, BF16) for constant in constants],
            pltpu.VMEM((members, 2, 3, channels // 2, lats // members * pad), BF16),
            pltpu.VMEM((lats, pad, LANES), BF16),
            pltpu.VMEM((chans * lats, pad, LANES), BF16),
            pltpu.VMEM((chans * lats, pad, LANES), BF16),
            pltpu.VMEM((lats, pad, LANES), BF16),
            pltpu.VMEM((pieces, piece, channels), BF16),
            pltpu.VMEM((pieces, piece, channels), BF16),
            pltpu.VMEM((pieces, piece, channels), BF16),
            dma((5,)),
            dma((3,)),
            dma((2,)),
            dma((2,)),
            dma((3,)),
            dma((2 + lats,)),
        ],
        compiler_params=pltpu.CompilerParams(
            collective_id=0, has_side_effects=True, vmem_limit_bytes=48 << 20
        ),
    )(*operands)
    result, weight = stored_whole(result, weight)
    return result.reshape(grad_out.shape), weight


def fits(mesh, rows, lon, channels):
    lats, chans, members = (mesh.shape[axis] for axis in ("lat", "chan", "ens"))
    return (
        members == 2 and chans == 2 and lats == 4 and rows * lon <= 512
        and lon % 16 == 0 and rows % 2 == 0
        and channels // chans == LANES + LANES // 2
        and channels % (members * lats * 16) == 0
    )


def solution(mesh):
    placed = (
        P(("grp", "ens"), "lat", None, "chan"),
        P(("grp", "ens"), "lat", None, "chan"),
        P(("grp", "ens"), ("lat", "chan"), None, None, None),
        P(("lat", "chan"), None, "ens"),
        P(),
    )

    def local(grad_out, *rest):
        rows, lon, cols = grad_out.shape[1:]
        small = fits(mesh, rows, lon, cols * mesh.shape["chan"])
        return (fused if small else on_device)(grad_out, *rest)

    return jax.shard_map(
        local,
        mesh=mesh,
        in_specs=placed,
        out_specs=(P(("grp", "ens"), "lat", None, "chan"), P("grp", None)),
        check_vma=False,
    )
```

```python
import math

import jax
import jax.numpy as jnp
import numpy as np
from jax import lax
from jax.experimental import pallas as pl
from jax.experimental.pallas import tpu as pltpu
from jax.sharding import PartitionSpec as P


def fourier_table(lon_count, mode_count):
    longitude = jnp.arange(lon_count, dtype=jnp.int32)[:, None]
    wavenumber = jnp.arange(mode_count, dtype=jnp.int32)[None, :]
    product_index = longitude * wavenumber % lon_count
    angles = 2.0 * math.pi / lon_count * product_index.astype(jnp.float32)
    factor = math.sqrt(2.0 / lon_count)
    stacked = jnp.stack([jnp.cos(angles), -jnp.sin(angles)], axis=2) * factor
    return stacked.reshape(lon_count, 2 * mode_count).astype(jnp.bfloat16)


def silu_backward(cotangent, preact):
    values = preact.astype(jnp.float32)
    gate_value = jax.nn.sigmoid(values)
    return (
        cotangent.astype(jnp.float32) * gate_value * (1.0 + values * (1.0 - gate_value))
    ).astype(jnp.bfloat16)


def on_device(grad_out, pre_act, coeffs, legendre, mixing):
    lat_rows = grad_out.shape[1]
    lon_count = grad_out.shape[2]
    chan_cols = grad_out.shape[3]
    mode_count = lon_count // 2
    lat_devices = lax.axis_size("lat")
    chan_count = lax.axis_size("chan")
    members = lax.axis_size("ens")
    lat_count = lat_rows * lat_devices
    channels = chan_cols * chan_count
    mode_width = 2 * mode_count // (lat_devices * chan_count)
    local_modes = mode_width // 2
    fourier = fourier_table(lon_count, mode_count)
    scaled = silu_backward(grad_out[0], pre_act[0])
    spectral = jnp.einsum(
        "nk,anc->akc", fourier, scaled, preferred_element_type=jnp.float32
    ).astype(jnp.bfloat16)
    exchanged = lax.all_to_all(
        lax.all_to_all(spectral, "lat", split_axis=1, concat_axis=0, tiled=True),
        "chan",
        split_axis=1,
        concat_axis=2,
        tiled=True,
    )
    spectral_modes = exchanged.reshape(lat_count, local_modes, 2, channels)
    legendre_full = lax.all_gather(legendre, "ens", axis=2, tiled=True)
    coef_grad = jnp.einsum(
        "mla,amrc->mlrc", legendre_full, spectral_modes, preferred_element_type=jnp.float32
    ).astype(jnp.bfloat16)
    stored = coeffs[0].reshape(-1, channels)
    flat_grad = coef_grad.reshape(-1, channels)
    weight_grad = lax.dot_general(
        stored, flat_grad, (((0,), (0,)), ((), ())), preferred_element_type=jnp.float32
    )
    weight_grad = weight_grad * (1.0 / (members * mode_count))
    weight_grad = lax.psum(weight_grad, ("lat", "chan", "ens"))
    mixed_grad = lax.dot_general(
        coef_grad, mixing, (((3,), (1,)), ((), ())), preferred_element_type=jnp.float32
    ).astype(jnp.bfloat16)
    returned = jnp.einsum(
        "mla,mlrc->amrc", legendre_full, mixed_grad, preferred_element_type=jnp.float32
    ).astype(jnp.bfloat16)
    shaped = returned.reshape(lat_count, 1, mode_width, channels)
    received = lax.all_to_all(
        lax.all_to_all(shaped, "lat", split_axis=0, concat_axis=1, tiled=True),
        "chan",
        split_axis=3,
        concat_axis=2,
        tiled=True,
    )
    row_coeffs = received.reshape(lat_rows, 2 * mode_count, chan_cols)
    spatial = jnp.einsum("nk,akc->anc", fourier, row_coeffs, preferred_element_type=jnp.float32)
    result = (grad_out[0].astype(jnp.float32) + spatial).astype(jnp.bfloat16)
    return (result[None], weight_grad)

MESH = pl.DeviceIdType.MESH
BF16 = jnp.bfloat16
F32 = jnp.float32


def dot(a, b, dims=((1,), (0,))):
    return lax.dot_general(a, b, (dims, ((), ())), preferred_element_type=F32)


LANES = 128


def slots(rows, width):
    whole = [(a, a, k) for a in range(rows) for k in range(width)]
    paired = [(a, a + 1, k) for a in range(0, rows, 2) for k in range(width)]
    return whole, paired


def padded(rows, width):
    return -(-(rows + rows // 2) * width // 16) * 16


def tables(rows, lon, lats, chans, members, modes, degrees):
    width = 2 * modes * chans
    pad = padded(rows, width)
    n = np.arange(lon)[:, None]
    m = np.arange(lon // 2)[None, :]
    angles = np.float32(2.0 * math.pi / lon) * (n * m % lon).astype(np.float32)
    table = np.stack([np.cos(angles), -np.sin(angles)], axis=2).reshape(lon, lon)
    table = (table * np.float32(math.sqrt(2.0 / lon))).astype(np.float32)
    groups = rows + rows // 2
    inverse = np.zeros((groups, lon, lats, pad), np.float32)
    for g in range(groups):
        for d in range(lats):
            inverse[g, :, d, g * width:(g + 1) * width] = table[:, d * width:(d + 1) * width]
    inverse = inverse.reshape(groups * lon, lats * pad)
    whole, paired = slots(rows, width)
    near = lats // members
    lat_of = np.full((3, near, pad), -1)
    key_of = np.full((near, pad), -1)
    for z in range(near):
        for i, (even, odd, k) in enumerate(whole + paired):
            key_of[z, i] = k
            kinds = ((0, even),) if i < len(whole) else ((1, even), (2, odd))
            for kind, lat in kinds:
                lat_of[kind, z, i] = z * rows + lat
    lat_of, key_of = lat_of.reshape(3, -1), key_of.reshape(-1)
    select = (lat_of[:, None, :] == np.arange(near * rows)[None, :, None]).astype(np.float32)
    row = np.arange(chans * modes * degrees * 2)
    spread = (np.arange(chans * modes * degrees)[:, None] == row[None, :] // 2).astype(np.float32)
    row_key = row // (2 * degrees) * 2 + row % 2
    mask = (row_key[:, None] == key_of[None, :]).astype(np.float32)
    width = lats * pad
    tables = [mask, mask.T, spread]
    tables += [np.pad(part, ((0, -part.shape[0] % 16), (0, 0))) for part in select]
    tables = [np.pad(part, ((0, 0), (0, width - part.shape[1]))) for part in tables + [inverse]]
    starts = np.cumsum([0] + [part.shape[0] for part in tables]).tolist()
    cast = lambda x: jnp.asarray(np.ascontiguousarray(x), BF16)
    return cast(inverse.T), cast(np.concatenate(tables, axis=0)), starts


def swap_halves(x):
    return pltpu.roll(x, LANES // 2, 1)


def lower_half(x):
    return lax.broadcasted_iota(jnp.int32, x.shape, 1) < LANES // 2


def joined(wide, even, odd):
    first, second = wide[:, :LANES], wide[:, LANES:]
    low = lower_half(first)
    none = jnp.zeros_like(first)
    middle = jnp.where(low, even[:, :LANES], none)
    middle = middle + swap_halves(jnp.where(low, second, odd[:, :LANES]))
    last = jnp.where(low, none, odd[:, LANES:])
    last = last + swap_halves(jnp.where(low, even[:, LANES:], second))
    return jnp.concatenate([first, middle, last], axis=1).astype(BF16)


def fused_kernel(
    lats, chans, members, lon, starts,
    grad_hbm, pre_hbm, coeffs_hbm, leg_hbm, mix_hbm, fwd_hbm, table_hbm,
    out_ref, weight_ref,
    point_ref, coeffs_ref, lbuf, mix_ref, fwd_ref, table_ref,
    terms, sbuf, rbuf, sbuf2, rbuf2, w1s, w1r, full_ref,
    isem, lsem, esem, ssem, rsem, gsem, go,
):
    z, c, x = lax.axis_index("lat"), lax.axis_index("chan"), lax.axis_index("ens")
    pad = rbuf.shape[1]
    half = lats // 2
    high = z // half
    other = lax.rem(x + 1, members)
    sibling = {"chan": 1 - c}
    mine = z * members + x
    pieces, piece = full_ref.shape[:2]
    modes, held, degrees = lbuf.shape[1:]
    points = point_ref.shape[1]
    last = pieces - 1
    double = last - members

    def home(q):
        return q - q // last * members

    count, near = 2 * chans * modes * degrees, half * pad
    early_first = sorted(
        ((a, b) for a in range(lats) for b in range(members)), key=lambda place: (sum(place), place)
    )

    def table(index, rows, cols):
        return table_ref[starts[index]:starts[index] + rows, :cols]

    def remote(src, dst, send, recv, target):
        return pltpu.make_async_remote_copy(
            src_ref=src, dst_ref=dst, send_sem=send, recv_sem=recv,
            device_id=target, device_id_type=MESH,
        )

    def done(ref, sem):
        pltpu.make_async_copy(ref, ref, sem).wait()

    far_first = [high * j + (1 - high) * (lats - 1 - j) for j in range(half)]
    far_first += [high * half + lax.rem(z + j, half) for j in range(1, half)]
    near_first = [z] + far_first[::-1]
    order = [(pz, px) for pz in near_first for px in (x, other)][1:]

    def load(source, target, index):
        return pltpu.make_async_copy(source, target, isem.at[index])

    urgent = load(fwd_hbm, fwd_ref, 1)
    shared = [load(leg_hbm, lbuf.at[x * chans + c], 2), load(table_hbm, table_ref, 3)]
    own_coeffs = load(coeffs_hbm, coeffs_ref.at[1], 4)
    own_mix = load(mix_hbm, mix_ref, 4)
    load(pre_hbm, point_ref.at[0], 0).start()
    load(grad_hbm, point_ref.at[1], 0).start()
    urgent.start()

    barrier = pltpu.get_barrier_semaphore()

    def announce(**target):
        pl.semaphore_signal(barrier, inc=1, device_id=target, device_id_type=MESH)

    @pl.when(c == 1)
    def _():
        for pz in far_first:
            for pc in (0, 1):
                announce(lat=pz, chan=pc)

    announce(ens=other, chan=c)
    announce(ens=other, chan=1 - c)
    announce(chan=1 - c)

    for copy in shared:
        copy.start()

    @pl.when(c == 0)
    def _():
        own_mix.start()

    @pl.when(c == 1)
    def _():
        own_coeffs.start()

    done(point_ref, isem.at[0])
    urgent.wait()
    values = point_ref[0].astype(F32)
    gate = jax.nn.sigmoid(values)
    scaled = point_ref[1].astype(F32) * gate * (1.0 + values * (1.0 - gate))
    tail = scaled[:, LANES:].reshape(-1, 2, lon, LANES // 2)
    paired = jnp.concatenate([tail[:, 0], tail[:, 1]], axis=-1).reshape(-1, LANES)
    packed = jnp.concatenate([scaled[:, :LANES], paired], axis=0).astype(BF16)
    sbuf[...] = dot(fwd_ref[...], packed).astype(BF16).reshape(lats, pad, LANES)

    pl.semaphore_wait(barrier, lats + members * chans - 2)

    leg = x * chans + c
    for px, pc, kind in ((other, c, 1), (other, 1 - c, 1), (x, 1 - c, 0)):
        remote(
            leg_hbm, lbuf.at[leg], lsem.at[0], lsem.at[1 + kind], {"ens": px, "chan": pc}
        ).start()
    for q in far_first:
        remote(
            sbuf.at[q], rbuf.at[c * lats + z], esem.at[0], esem.at[1], {"lat": q, "chan": 1}
        ).start()

    def transform(px):
        row = [lbuf[px * chans + pc, m].astype(F32) for pc in range(chans) for m in range(modes)]
        spread = table(2, count // 2, count)
        maps = dot(jnp.concatenate(row, axis=1).astype(BF16), spread).astype(BF16)
        down = ((0,), (0,))
        analysis = [
            dot(maps, table(3 + v, held, near), down).astype(BF16) * table(0, count, near)
            for v in range(3)
        ]
        return maps, analysis

    def maps_here():
        for copy in shared:
            copy.wait()
        done(lbuf.at[x * chans + 1 - c], lsem.at[1])

    def maps_there():
        done(lbuf.at[pl.ds(other * chans, chans)], lsem.at[2])

    def received(px):
        return jnp.concatenate(
            [rbuf[pl.ds(h * lats + px * half, half)].reshape(-1, LANES) for h in range(chans)],
            axis=1,
        )

    def back_to_grid():
        inverse = table(6, points + points // 2, lats * pad)
        spatial = dot(inverse, rbuf2[...].reshape(lats * pad, LANES))
        pairs = spatial[points:].reshape(-1, 1, lon, LANES)
        low, up = pairs[..., :LANES // 2], pairs[..., LANES // 2:]
        rest = jnp.concatenate([low, up], axis=1).reshape(points, LANES // 2)
        spatial = jnp.concatenate([spatial[:points], rest], axis=1)
        out_ref[...] = (point_ref[1].astype(F32) + spatial).astype(BF16)

    mean = 1.0 / (members * lon // 2)

    def average(pz):
        start = pz * members * piece
        rows = pl.ds(pl.multiple_of(start, members * piece), members * piece)
        value = full_ref[pl.ds(pz * members, members)].astype(F32) * mean
        weight_ref[rows, :] = value.reshape(members * piece, value.shape[2])

    @pl.when(c == 0)
    def _():
        passed = remote(coeffs_hbm, coeffs_ref.at[0], ssem.at[0], ssem.at[1], sibling)
        passed.start()
        remote(
            sbuf.at[z], rbuf.at[c * lats + z], esem.at[0], esem.at[1], sibling
        ).start()
        maps_here()
        near_maps, near_down = transform(x)
        own_mix.wait()

        def upward(maps):
            down = ((0,), (0,))
            return [
                dot(table(3 + v, held, near), maps, down).astype(BF16) * table(1, near, count)
                for v in range(3)
            ]

        near_up = upward(near_maps)
        maps_there()
        far_maps, far_down = transform(other)
        far_up = upward(far_maps)
        done(rbuf, ssem.at[1])
        block = received(x), received(other)
        coef = joined(*(dot(near_down[v], block[0]) + dot(far_down[v], block[1]) for v in range(3)))
        mixed = dot(coef, mix_ref[...], ((1,), (1,)))
        t0, t1, t2 = (mixed[:, i * LANES:(i + 1) * LANES] for i in range(3))
        low = lower_half(t0)
        none = jnp.zeros_like(t0)
        even0, odd1 = jnp.where(low, t1, none), jnp.where(low, none, t2)
        sides = (
            (t0, swap_halves(jnp.where(low, t2, t1))),
            (even0, swap_halves(odd1)),
            (swap_halves(even0), odd1),
        )
        sides = [jnp.concatenate(side, axis=1).astype(BF16) for side in sides]
        for px, synthesis in ((other, far_up), (x, near_up)):
            back = sum(dot(matrix, side) for matrix, side in zip(synthesis, sides)).astype(BF16)
            for h in range(chans):
                part = back[:, h * LANES:(h + 1) * LANES].reshape(half, pad, LANES)
                sbuf2[pl.ds(h * lats + px * half, half)] = part
        def send_home(q):
            for h in range(chans):
                remote(
                    sbuf2.at[h * lats + q], rbuf2.at[z], rsem.at[0], rsem.at[2],
                    {"lat": q, "chan": h},
                ).start()

        pl.when(z > 0)(lambda: send_home(0))
        pl.semaphore_wait(go, 1)
        pl.when(z == 0)(lambda: send_home(1))
        for j in range(1, lats - 1):
            send_home(j + 1 - (z + lats - 1 - j) // lats)
        remote(sbuf2.at[lats + z], rbuf2.at[z], rsem.at[0], rsem.at[2], sibling).start()
        rbuf2[z] = sbuf2[z]
        done(rbuf2.at[pl.ds(0, lats - 1)], rsem.at[2])
        back_to_grid()
        for pz in near_first:
            done(full_ref.at[pl.ds(pz * members, members)], gsem.at[2 + pz])
            average(pz)
        passed.wait_send()
        done(sbuf, esem.at[0])
        done(sbuf2.at[pl.ds(0, chans * lats - 1)], rsem.at[0])

    @pl.when(c == 1)
    def _():
        rbuf[lats + z] = sbuf[z]
        own_coeffs.wait()
        done(coeffs_ref.at[0], ssem.at[1])
        flat = coeffs_ref[...].reshape(-1, coeffs_ref.shape[-1])
        stored = flat.astype(F32).T.astype(BF16)
        maps_here()
        for px in (x, other):
            if px is other:
                maps_there()
            _, analysis = transform(px)
            for v in range(3):
                value = dot(stored, analysis[v]).astype(BF16)
                terms[px, :, v] = value.reshape(2, -1, value.shape[1])

        done(rbuf.at[pl.ds(0, chans * lats - 1)], esem.at[1])
        block = remote(rbuf, rbuf, ssem.at[0], ssem.at[1], sibling)
        block.start()
        arrays = received(0), received(1)
        for group, targets in ((1 - high, far_first[:half]), (high, far_first[half:] + [z])):
            value = joined(*(
                dot(terms[0, group, v], arrays[0]) + dot(terms[1, group, v], arrays[1])
                for v in range(3)
            ))
            share = half * members
            w1s[pl.ds(group * share, share)] = value.reshape(share, piece, value.shape[1])
            for pz in targets:
                for px in (other, x):
                    q = pz * members + px
                    copy = remote(
                        w1s.at[q], w1r.at[q // last * pieces + mine], rsem.at[0],
                        rsem.at[1 + 2 * (q // last)], {"lat": home(q) // members, "ens": px},
                    )
                    pl.when(home(q) != mine)(copy.start)

        @pl.when(mine == last)
        def _():
            done(w1s, rsem.at[0])

        @pl.when(mine == double)
        def _():
            done(w1s.at[pl.ds(0, pieces - 2)], rsem.at[0])

        @pl.when(jnp.logical_and(mine != last, mine != double))
        def _():
            done(w1s.at[pl.ds(0, pieces - 1)], rsem.at[0])

        pl.semaphore_signal(go, inc=1, device_id=sibling, device_id_type=MESH)

        def reduced(slot, index):
            start = slot * pieces
            done(w1r.at[pl.ds(start, pieces - 1)], rsem.at[1 + 2 * slot])
            total = w1s[index].astype(F32)
            for pz, px in order:
                total = total + w1r[start + pz * members + px].astype(F32)
            full_ref[index] = total.astype(BF16)

        @pl.when(mine != last)
        def _():
            reduced(0, mine)

        @pl.when(mine == double)
        def _():
            reduced(1, last)

        for pz, px in early_first:
            target = {"lat": pz, "ens": px}
            away = pz * members + px != mine
            first = remote(
                full_ref.at[mine], full_ref.at[mine], gsem.at[0], gsem.at[2 + z], target
            )
            second = remote(
                full_ref.at[last], full_ref.at[last], gsem.at[0], gsem.at[1 + lats], target
            )
            pl.when(jnp.logical_and(away, mine != last))(first.start)
            pl.when(jnp.logical_and(away, mine == double))(second.start)
        for pz in near_first:
            both = full_ref.at[pl.ds(pz * members, members)]
            one = full_ref.at[pz * members + other]
            if pz is z:
                single = mine != last
            else:
                single = jnp.logical_and(mine == double, pz == lats - 1)

            @pl.when(single)
            def _():
                done(one, gsem.at[2 + pz])

            @pl.when(jnp.logical_not(single))
            def _():
                done(both, gsem.at[2 + pz])

            remote(both, both, gsem.at[1], gsem.at[2 + pz], sibling).start()
            average(pz)
        done(rbuf2, rsem.at[2])
        back_to_grid()
        block.wait_send()
        done(sbuf.at[pl.ds(0, lats - 1)], esem.at[0])

        @pl.when(mine == double)
        def _():
            done(w1r.at[pl.ds(0, 2 * pieces - 2)], gsem.at[0])

        @pl.when(jnp.logical_and(mine != last, mine != double))
        def _():
            done(full_ref.at[pl.ds(0, pieces - 1)], gsem.at[0])

        done(full_ref, gsem.at[1])

    done(lbuf.at[pl.ds(0, members * chans - 1)], lsem.at[0])


def store_kernel(result, weight, result_hbm, weight_hbm, sems):
    stores = [
        pltpu.make_async_copy(weight, weight_hbm, sems.at[0]),
        pltpu.make_async_copy(result, result_hbm, sems.at[1]),
    ]
    for store in stores:
        store.start()
    for store in stores:
        store.wait()


def stored_whole(result, weight):
    return pl.pallas_call(
        store_kernel,
        out_shape=tuple(jax.ShapeDtypeStruct(x.shape, x.dtype) for x in (result, weight)),
        in_specs=[pl.BlockSpec(memory_space=pl.ANY)] * 2,
        out_specs=(pl.BlockSpec(memory_space=pltpu.HBM),) * 2,
        scratch_shapes=[pltpu.SemaphoreType.DMA((2,))],
        compiler_params=pltpu.CompilerParams(vmem_limit_bytes=1 << 20),
    )(result, weight)


def fused(grad_out, pre_act, coeffs, legendre, mixing):
    rows, lon, cols = grad_out.shape[1:]
    lats, chans = lax.axis_size("lat"), lax.axis_size("chan")
    members = lax.axis_size("ens")
    modes, degrees, held = legendre.shape
    channels = cols * chans
    pad = padded(rows, 2 * modes * chans)
    pieces = lats * members
    piece = channels // pieces
    *constants, starts = tables(rows, lon, lats, chans, members, modes, degrees)
    dma = pltpu.SemaphoreType.DMA

    def kernel(*refs):
        fused_kernel(lats, chans, members, lon, starts, *refs)

    operands = (
        grad_out.reshape(rows * lon, cols),
        pre_act.reshape(rows * lon, cols),
        coeffs.reshape(modes * degrees, 2, channels),
        legendre.transpose(0, 2, 1),
        mixing,
        *constants,
    )
    operands = tuple(pltpu.with_memory_space_constraint(x, pltpu.HBM) for x in operands)
    result, weight = pl.pallas_call(
        kernel,
        out_shape=(
            pltpu.VMEM((rows * lon, cols), BF16),
            pltpu.VMEM((channels, channels), F32),
        ),
        in_specs=[pl.BlockSpec(memory_space=pltpu.HBM)] * len(operands),
        out_specs=(pl.BlockSpec(memory_space=pltpu.VMEM),) * 2,
        scratch_shapes=[
            pltpu.VMEM((2, rows * lon, cols), BF16),
            pltpu.VMEM((chans, modes * degrees, 2, channels), BF16),
            pltpu.VMEM((members * chans, modes, held, degrees), BF16),
            pltpu.VMEM(mixing.shape, BF16),
            *[pltpu.VMEM(constant.shape, BF16) for constant in constants],
            pltpu.VMEM((members, 2, 3, channels // 2, lats // members * pad), BF16),
            pltpu.VMEM((lats, pad, LANES), BF16),
            pltpu.VMEM((chans * lats, pad, LANES), BF16),
            pltpu.VMEM((chans * lats, pad, LANES), BF16),
            pltpu.VMEM((lats, pad, LANES), BF16),
            pltpu.VMEM((pieces, piece, channels), BF16),
            pltpu.VMEM((2 * pieces, piece, channels), BF16),
            pltpu.VMEM((pieces, piece, channels), BF16),
            dma((5,)),
            dma((3,)),
            dma((2,)),
            dma((2,)),
            dma((4,)),
            dma((2 + lats,)),
            pltpu.SemaphoreType.REGULAR,
        ],
        compiler_params=pltpu.CompilerParams(
            collective_id=0, has_side_effects=True, vmem_limit_bytes=48 << 20
        ),
    )(*operands)
    result, weight = stored_whole(result, weight)
    return result.reshape(grad_out.shape), weight


def fits(mesh, rows, lon, channels):
    lats, chans, members = (mesh.shape[axis] for axis in ("lat", "chan", "ens"))
    return (
        members == 2 and chans == 2 and lats == 4 and rows * lon <= 512
        and lon % 16 == 0 and rows % 2 == 0
        and channels // chans == LANES + LANES // 2
        and channels % (members * lats * 16) == 0
    )


def solution(mesh):
    placed = (
        P(("grp", "ens"), "lat", None, "chan"),
        P(("grp", "ens"), "lat", None, "chan"),
        P(("grp", "ens"), ("lat", "chan"), None, None, None),
        P(("lat", "chan"), None, "ens"),
        P(),
    )

    def local(grad_out, *rest):
        rows, lon, cols = grad_out.shape[1:]
        small = fits(mesh, rows, lon, cols * mesh.shape["chan"])
        return (fused if small else on_device)(grad_out, *rest)

    return jax.shard_map(
        local,
        mesh=mesh,
        in_specs=placed,
        out_specs=(P(("grp", "ens"), "lat", None, "chan"), P("grp", None)),
        check_vma=False,
    )
```

```python
import math

import jax
import jax.numpy as jnp
import numpy as np
from jax import lax
from jax.experimental import pallas as pl
from jax.experimental.pallas import tpu as pltpu
from jax.sharding import PartitionSpec as P


def fourier_table(lon_count, mode_count):
    longitude = jnp.arange(lon_count, dtype=jnp.int32)[:, None]
    wavenumber = jnp.arange(mode_count, dtype=jnp.int32)[None, :]
    product_index = longitude * wavenumber % lon_count
    angles = 2.0 * math.pi / lon_count * product_index.astype(jnp.float32)
    factor = math.sqrt(2.0 / lon_count)
    stacked = jnp.stack([jnp.cos(angles), -jnp.sin(angles)], axis=2) * factor
    return stacked.reshape(lon_count, 2 * mode_count).astype(jnp.bfloat16)


def silu_backward(cotangent, preact):
    values = preact.astype(jnp.float32)
    gate_value = jax.nn.sigmoid(values)
    return (
        cotangent.astype(jnp.float32) * gate_value * (1.0 + values * (1.0 - gate_value))
    ).astype(jnp.bfloat16)


def on_device(grad_out, pre_act, coeffs, legendre, mixing):
    lat_rows = grad_out.shape[1]
    lon_count = grad_out.shape[2]
    chan_cols = grad_out.shape[3]
    mode_count = lon_count // 2
    lat_devices = lax.axis_size("lat")
    chan_count = lax.axis_size("chan")
    members = lax.axis_size("ens")
    lat_count = lat_rows * lat_devices
    channels = chan_cols * chan_count
    mode_width = 2 * mode_count // (lat_devices * chan_count)
    local_modes = mode_width // 2
    fourier = fourier_table(lon_count, mode_count)
    scaled = silu_backward(grad_out[0], pre_act[0])
    spectral = jnp.einsum(
        "nk,anc->akc", fourier, scaled, preferred_element_type=jnp.float32
    ).astype(jnp.bfloat16)
    exchanged = lax.all_to_all(
        lax.all_to_all(spectral, "lat", split_axis=1, concat_axis=0, tiled=True),
        "chan",
        split_axis=1,
        concat_axis=2,
        tiled=True,
    )
    spectral_modes = exchanged.reshape(lat_count, local_modes, 2, channels)
    legendre_full = lax.all_gather(legendre, "ens", axis=2, tiled=True)
    coef_grad = jnp.einsum(
        "mla,amrc->mlrc", legendre_full, spectral_modes, preferred_element_type=jnp.float32
    ).astype(jnp.bfloat16)
    stored = coeffs[0].reshape(-1, channels)
    flat_grad = coef_grad.reshape(-1, channels)
    weight_grad = lax.dot_general(
        stored, flat_grad, (((0,), (0,)), ((), ())), preferred_element_type=jnp.float32
    )
    weight_grad = weight_grad * (1.0 / (members * mode_count))
    weight_grad = lax.psum(weight_grad, ("lat", "chan", "ens"))
    mixed_grad = lax.dot_general(
        coef_grad, mixing, (((3,), (1,)), ((), ())), preferred_element_type=jnp.float32
    ).astype(jnp.bfloat16)
    returned = jnp.einsum(
        "mla,mlrc->amrc", legendre_full, mixed_grad, preferred_element_type=jnp.float32
    ).astype(jnp.bfloat16)
    shaped = returned.reshape(lat_count, 1, mode_width, channels)
    received = lax.all_to_all(
        lax.all_to_all(shaped, "lat", split_axis=0, concat_axis=1, tiled=True),
        "chan",
        split_axis=3,
        concat_axis=2,
        tiled=True,
    )
    row_coeffs = received.reshape(lat_rows, 2 * mode_count, chan_cols)
    spatial = jnp.einsum("nk,akc->anc", fourier, row_coeffs, preferred_element_type=jnp.float32)
    result = (grad_out[0].astype(jnp.float32) + spatial).astype(jnp.bfloat16)
    return (result[None], weight_grad)

MESH = pl.DeviceIdType.MESH
BF16 = jnp.bfloat16
F32 = jnp.float32


def dot(a, b, dims=((1,), (0,))):
    return lax.dot_general(a, b, (dims, ((), ())), preferred_element_type=F32)


LANES = 128


def slots(rows, width):
    whole = [(a, a, k) for a in range(rows) for k in range(width)]
    paired = [(a, a + 1, k) for a in range(0, rows, 2) for k in range(width)]
    return whole, paired


def padded(rows, width):
    return -(-(rows + rows // 2) * width // 16) * 16


def tables(rows, lon, lats, chans, members, modes, degrees):
    width = 2 * modes * chans
    pad = padded(rows, width)
    n = np.arange(lon)[:, None]
    m = np.arange(lon // 2)[None, :]
    angles = np.float32(2.0 * math.pi / lon) * (n * m % lon).astype(np.float32)
    table = np.stack([np.cos(angles), -np.sin(angles)], axis=2).reshape(lon, lon)
    table = (table * np.float32(math.sqrt(2.0 / lon))).astype(np.float32)
    groups = rows + rows // 2
    inverse = np.zeros((groups, lon, lats, pad), np.float32)
    for g in range(groups):
        for d in range(lats):
            inverse[g, :, d, g * width:(g + 1) * width] = table[:, d * width:(d + 1) * width]
    inverse = inverse.reshape(groups * lon, lats * pad)
    whole, paired = slots(rows, width)
    near = lats // members
    lat_of = np.full((3, near, pad), -1)
    key_of = np.full((near, pad), -1)
    for z in range(near):
        for i, (even, odd, k) in enumerate(whole + paired):
            key_of[z, i] = k
            kinds = ((0, even),) if i < len(whole) else ((1, even), (2, odd))
            for kind, lat in kinds:
                lat_of[kind, z, i] = z * rows + lat
    lat_of, key_of = lat_of.reshape(3, -1), key_of.reshape(-1)
    select = (lat_of[:, None, :] == np.arange(near * rows)[None, :, None]).astype(np.float32)
    row = np.arange(chans * modes * degrees * 2)
    spread = (np.arange(chans * modes * degrees)[:, None] == row[None, :] // 2).astype(np.float32)
    row_key = row // (2 * degrees) * 2 + row % 2
    mask = (row_key[:, None] == key_of[None, :]).astype(np.float32)
    width = lats * pad
    tables = [mask, mask.T, spread]
    tables += [np.pad(part, ((0, -part.shape[0] % 16), (0, 0))) for part in select]
    tables = [np.pad(part, ((0, 0), (0, width - part.shape[1]))) for part in tables + [inverse]]
    starts = np.cumsum([0] + [part.shape[0] for part in tables]).tolist()
    cast = lambda x: jnp.asarray(np.ascontiguousarray(x), BF16)
    return cast(inverse.T), cast(np.concatenate(tables, axis=0)), starts


def swap_halves(x):
    return pltpu.roll(x, LANES // 2, 1)


def lower_half(x):
    return lax.broadcasted_iota(jnp.int32, x.shape, 1) < LANES // 2


def joined(wide, even, odd):
    first, second = wide[:, :LANES], wide[:, LANES:]
    low = lower_half(first)
    none = jnp.zeros_like(first)
    middle = jnp.where(low, even[:, :LANES], none)
    middle = middle + swap_halves(jnp.where(low, second, odd[:, :LANES]))
    last = jnp.where(low, none, odd[:, LANES:])
    last = last + swap_halves(jnp.where(low, even[:, LANES:], second))
    return jnp.concatenate([first, middle, last], axis=1).astype(BF16)


def parted(wide, even, odd):
    low = lower_half(even[:, :LANES])
    rest = jnp.where(low, even[:, :LANES], odd[:, LANES:])
    rest = rest + swap_halves(jnp.where(low, even[:, LANES:], odd[:, :LANES]))
    return jnp.concatenate([wide, rest], axis=1).astype(BF16)


def in_order(parts):
    first, second, rest = (parts[:, i * LANES:(i + 1) * LANES] for i in range(3))
    low, second = lower_half(first), swap_halves(second)
    return jnp.concatenate(
        [first, jnp.where(low, rest, second), jnp.where(low, second, rest)], axis=1
    )


def fused_kernel(
    lats, chans, members, lon, starts,
    grad_hbm, pre_hbm, coeffs_hbm, leg_hbm, mix_hbm, fwd_hbm, table_hbm,
    out_ref, weight_ref,
    point_ref, coeffs_ref, lbuf, mix_ref, fwd_ref, table_ref,
    terms, sbuf, rbuf, sbuf2, rbuf2, w1s, w1r, full_ref,
    isem, lsem, esem, ssem, rsem, gsem, go,
):
    z, c, x = lax.axis_index("lat"), lax.axis_index("chan"), lax.axis_index("ens")
    pad = rbuf.shape[1]
    half = lats // 2
    high = z // half
    other = lax.rem(x + 1, members)
    sibling = {"chan": 1 - c}
    mine = z * members + x
    pieces, piece = full_ref.shape[:2]
    modes, held, degrees = lbuf.shape[1:]
    points = point_ref.shape[1]
    last = pieces - 1
    double = last - members

    def home(q):
        return q - q // last * members

    count, near = 2 * chans * modes * degrees, half * pad
    early_first = sorted(
        ((a, b) for a in range(lats) for b in range(members)), key=lambda place: (sum(place), place)
    )

    def table(index, rows, cols):
        return table_ref[starts[index]:starts[index] + rows, :cols]

    def remote(src, dst, send, recv, target):
        return pltpu.make_async_remote_copy(
            src_ref=src, dst_ref=dst, send_sem=send, recv_sem=recv,
            device_id=target, device_id_type=MESH,
        )

    def done(ref, sem):
        pltpu.make_async_copy(ref, ref, sem).wait()

    far_first = [high * j + (1 - high) * (lats - 1 - j) for j in range(half)]
    far_first += [high * half + lax.rem(z + j, half) for j in range(1, half)]
    near_first = [z] + far_first[::-1]
    order = [(pz, px) for pz in near_first for px in (x, other)][1:]

    def load(source, target, index):
        return pltpu.make_async_copy(source, target, isem.at[index])

    urgent = load(fwd_hbm, fwd_ref, 1)
    shared = [load(leg_hbm, lbuf.at[x * chans + c], 2), load(table_hbm, table_ref, 3)]
    own_coeffs = load(coeffs_hbm, coeffs_ref.at[1], 4)
    own_mix = load(mix_hbm, mix_ref, 4)
    load(pre_hbm, point_ref.at[0], 0).start()
    load(grad_hbm, point_ref.at[1], 0).start()
    quarter = fwd_ref.shape[0] // lats
    for i in range(lats):
        rows = pl.ds(i * quarter, quarter)
        load(fwd_hbm.at[rows], fwd_ref.at[rows], 1).start()

    barrier = pltpu.get_barrier_semaphore()

    def announce(**target):
        pl.semaphore_signal(barrier, inc=1, device_id=target, device_id_type=MESH)

    @pl.when(c == 1)
    def _():
        for pz in far_first:
            for pc in (0, 1):
                announce(lat=pz, chan=pc)

    announce(ens=other, chan=c)
    announce(ens=other, chan=1 - c)
    announce(chan=1 - c)

    for copy in shared:
        copy.start()

    @pl.when(c == 0)
    def _():
        own_mix.start()

    @pl.when(c == 1)
    def _():
        own_coeffs.start()

    done(point_ref, isem.at[0])
    values = point_ref[0].astype(F32)
    gate = jax.nn.sigmoid(values)
    scaled = point_ref[1].astype(F32) * gate * (1.0 + values * (1.0 - gate))
    tail = scaled[:, LANES:].reshape(-1, 2, lon, LANES // 2)
    paired = jnp.concatenate([tail[:, 0], tail[:, 1]], axis=-1).reshape(-1, LANES)
    packed = jnp.concatenate([scaled[:, :LANES], paired], axis=0).astype(BF16)
    urgent.wait()
    sbuf[...] = dot(fwd_ref[...], packed).astype(BF16).reshape(lats, pad, LANES)

    pl.semaphore_wait(barrier, lats + members * chans - 2)

    leg = x * chans + c
    for px, pc, kind in ((other, c, 1), (other, 1 - c, 1), (x, 1 - c, 0)):
        remote(
            leg_hbm, lbuf.at[leg], lsem.at[0], lsem.at[1 + kind], {"ens": px, "chan": pc}
        ).start()
    for q in far_first:
        remote(
            sbuf.at[q], rbuf.at[c * lats + z], esem.at[0], esem.at[1], {"lat": q, "chan": 1}
        ).start()

    def transform(px):
        row = [lbuf[px * chans + pc, m].astype(F32) for pc in range(chans) for m in range(modes)]
        spread = table(2, count // 2, count)
        maps = dot(jnp.concatenate(row, axis=1).astype(BF16), spread).astype(BF16)
        down = ((0,), (0,))
        analysis = [
            dot(maps, table(3 + v, held, near), down).astype(BF16) * table(0, count, near)
            for v in range(3)
        ]
        return maps, analysis

    def maps_here():
        for copy in shared:
            copy.wait()
        done(lbuf.at[x * chans + 1 - c], lsem.at[1])

    def maps_there():
        done(lbuf.at[pl.ds(other * chans, chans)], lsem.at[2])

    def received(px):
        return jnp.concatenate(
            [rbuf[pl.ds(h * lats + px * half, half)].reshape(-1, LANES) for h in range(chans)],
            axis=1,
        )

    def back_to_grid():
        inverse = table(6, points + points // 2, lats * pad)
        spatial = dot(inverse, rbuf2[...].reshape(lats * pad, LANES))
        pairs = spatial[points:].reshape(-1, 1, lon, LANES)
        low, up = pairs[..., :LANES // 2], pairs[..., LANES // 2:]
        rest = jnp.concatenate([low, up], axis=1).reshape(points, LANES // 2)
        spatial = jnp.concatenate([spatial[:points], rest], axis=1)
        out_ref[...] = (point_ref[1].astype(F32) + spatial).astype(BF16)

    mean = 1.0 / (members * lon // 2)

    def average(pz):
        start = pz * members * piece
        rows = pl.ds(pl.multiple_of(start, members * piece), members * piece)
        value = full_ref[pl.ds(pz * members, members)].astype(F32) * mean
        weight_ref[rows, :] = in_order(value.reshape(members * piece, value.shape[2]))

    @pl.when(c == 0)
    def _():
        passed = remote(coeffs_hbm, coeffs_ref.at[0], ssem.at[0], ssem.at[1], sibling)
        passed.start()
        remote(
            sbuf.at[z], rbuf.at[c * lats + z], esem.at[0], esem.at[1], sibling
        ).start()
        maps_here()
        maps_there()
        own_mix.wait()
        analysis, synthesis = [], []
        for px in range(members):
            maps, down = transform(px)
            analysis.append(down)
            synthesis.append([
                dot(table(3 + v, held, near), maps, ((0,), (0,))).astype(BF16)
                * table(1, near, count)
                for v in range(3)
            ])
        done(rbuf, ssem.at[1])
        block = received(0), received(1)
        coef = joined(*(
            dot(analysis[0][v], block[0]) + dot(analysis[1][v], block[1]) for v in range(3)
        ))
        mixed = dot(coef, mix_ref[...], ((1,), (1,)))
        t0, t1, t2 = (mixed[:, i * LANES:(i + 1) * LANES] for i in range(3))
        low = lower_half(t0)
        none = jnp.zeros_like(t0)
        even0, odd1 = jnp.where(low, t1, none), jnp.where(low, none, t2)
        sides = (
            (t0, swap_halves(jnp.where(low, t2, t1))),
            (even0, swap_halves(odd1)),
            (swap_halves(even0), odd1),
        )
        sides = [jnp.concatenate(side, axis=1).astype(BF16) for side in sides]

        def send_home(q):
            for h in range(chans):
                remote(
                    sbuf2.at[h * lats + q], rbuf2.at[z], rsem.at[0], rsem.at[2],
                    {"lat": q, "chan": h},
                ).start()

        for px in range(members):
            back = sum(dot(matrix, side) for matrix, side in zip(synthesis[px], sides)).astype(BF16)
            for h in range(chans):
                part = back[:, h * LANES:(h + 1) * LANES].reshape(half, pad, LANES)
                sbuf2[h * lats + px * half:h * lats + (px + 1) * half] = part
            if px == 0:
                pl.when(z > 0)(lambda: send_home(0))
            else:
                pl.when(z == 0)(lambda: send_home(lats - 1))
        pl.semaphore_wait(go, 1)
        for j in range(1, lats - 1):
            send_home(j + jnp.where(jnp.logical_and(z > 0, z <= j), 1, 0))
        remote(sbuf2.at[lats + z], rbuf2.at[z], rsem.at[0], rsem.at[2], sibling).start()
        rbuf2[z] = sbuf2[z]
        passed.wait_send()
        done(sbuf, esem.at[0])
        done(lbuf.at[pl.ds(0, members * chans - 1)], lsem.at[0])
        done(rbuf2.at[pl.ds(0, lats - 1)], rsem.at[2])
        back_to_grid()
        done(sbuf2.at[pl.ds(0, chans * lats - 1)], rsem.at[0])
        for pz in near_first:
            done(full_ref.at[pl.ds(pz * members, members)], gsem.at[2 + pz])
            average(pz)

    @pl.when(c == 1)
    def _():
        rbuf[lats + z] = sbuf[z]
        own_coeffs.wait()
        done(coeffs_ref.at[0], ssem.at[1])
        flat = coeffs_ref[...].reshape(-1, coeffs_ref.shape[-1])
        stored = flat.astype(F32).T.astype(BF16)
        maps_here()
        for px in (x, other):
            if px is other:
                maps_there()
            _, analysis = transform(px)
            for v in range(3):
                value = dot(stored, analysis[v]).astype(BF16)
                terms[px, :, v] = value.reshape(2, -1, value.shape[1])

        done(rbuf.at[pl.ds(0, chans * lats - 1)], esem.at[1])
        block = remote(rbuf, rbuf, ssem.at[0], ssem.at[1], sibling)
        block.start()
        arrays = received(0), received(1)
        for group, targets in ((1 - high, far_first[:half]), (high, far_first[half:] + [z])):
            value = parted(*(
                dot(terms[0, group, v], arrays[0]) + dot(terms[1, group, v], arrays[1])
                for v in range(3)
            ))
            share = half * members
            w1s[pl.ds(group * share, share)] = value.reshape(share, piece, value.shape[1])
            for pz in targets:
                for px in (other, x):
                    q = pz * members + px
                    copy = remote(
                        w1s.at[q], w1r.at[q // last * pieces + mine], rsem.at[0],
                        rsem.at[1 + 2 * (q // last)], {"lat": home(q) // members, "ens": px},
                    )
                    pl.when(home(q) != mine)(copy.start)

        @pl.when(mine == last)
        def _():
            done(w1s, rsem.at[0])

        @pl.when(mine == double)
        def _():
            done(w1s.at[pl.ds(0, pieces - 2)], rsem.at[0])

        @pl.when(jnp.logical_and(mine != last, mine != double))
        def _():
            done(w1s.at[pl.ds(0, pieces - 1)], rsem.at[0])

        pl.semaphore_signal(go, inc=1, device_id=sibling, device_id_type=MESH)

        block.wait_send()
        done(sbuf.at[pl.ds(0, lats - 1)], esem.at[0])
        done(lbuf.at[pl.ds(0, members * chans - 1)], lsem.at[0])

        def reduced(slot, index):
            start = slot * pieces
            done(w1r.at[pl.ds(start, pieces - 1)], rsem.at[1 + 2 * slot])
            total = w1s[index].astype(F32)
            for pz, px in order:
                total = total + w1r[start + pz * members + px].astype(F32)
            full_ref[index] = total.astype(BF16)

        @pl.when(mine != last)
        def _():
            reduced(0, mine)

        @pl.when(mine == double)
        def _():
            reduced(1, last)

        for pz, px in early_first:
            target = {"lat": pz, "ens": px}
            away = pz * members + px != mine
            first = remote(
                full_ref.at[mine], full_ref.at[mine], gsem.at[0], gsem.at[2 + z], target
            )
            second = remote(
                full_ref.at[last], full_ref.at[last], gsem.at[0], gsem.at[1 + lats], target
            )
            pl.when(jnp.logical_and(away, mine != last))(first.start)
            pl.when(jnp.logical_and(away, mine == double))(second.start)
        for pz in near_first:
            both = full_ref.at[pl.ds(pz * members, members)]
            one = full_ref.at[pz * members + other]
            if pz is z:
                single = mine != last
            else:
                single = jnp.logical_and(mine == double, pz == lats - 1)

            @pl.when(single)
            def _():
                done(one, gsem.at[2 + pz])

            @pl.when(jnp.logical_not(single))
            def _():
                done(both, gsem.at[2 + pz])

            remote(both, both, gsem.at[1], gsem.at[2 + pz], sibling).start()
            average(pz)
        done(rbuf2, rsem.at[2])
        back_to_grid()

        @pl.when(mine == double)
        def _():
            done(w1r.at[pl.ds(0, 2 * pieces - 2)], gsem.at[0])

        @pl.when(jnp.logical_and(mine != last, mine != double))
        def _():
            done(full_ref.at[pl.ds(0, pieces - 1)], gsem.at[0])

        done(full_ref, gsem.at[1])


def store_kernel(result, weight, result_hbm, weight_hbm, sems):
    stores = [
        pltpu.make_async_copy(weight, weight_hbm, sems.at[0]),
        pltpu.make_async_copy(result, result_hbm, sems.at[1]),
    ]
    for store in stores:
        store.start()
    for store in stores:
        store.wait()


def stored_whole(result, weight):
    return pl.pallas_call(
        store_kernel,
        out_shape=tuple(jax.ShapeDtypeStruct(x.shape, x.dtype) for x in (result, weight)),
        in_specs=[pl.BlockSpec(memory_space=pl.ANY)] * 2,
        out_specs=(pl.BlockSpec(memory_space=pltpu.HBM),) * 2,
        scratch_shapes=[pltpu.SemaphoreType.DMA((2,))],
        compiler_params=pltpu.CompilerParams(vmem_limit_bytes=1 << 20),
    )(result, weight)


def fused(grad_out, pre_act, coeffs, legendre, mixing):
    rows, lon, cols = grad_out.shape[1:]
    lats, chans = lax.axis_size("lat"), lax.axis_size("chan")
    members = lax.axis_size("ens")
    modes, degrees, held = legendre.shape
    channels = cols * chans
    pad = padded(rows, 2 * modes * chans)
    pieces = lats * members
    piece = channels // pieces
    *constants, starts = tables(rows, lon, lats, chans, members, modes, degrees)
    dma = pltpu.SemaphoreType.DMA

    def kernel(*refs):
        fused_kernel(lats, chans, members, lon, starts, *refs)

    operands = (
        grad_out.reshape(rows * lon, cols),
        pre_act.reshape(rows * lon, cols),
        coeffs.reshape(modes * degrees, 2, channels),
        legendre.transpose(0, 2, 1),
        mixing,
        *constants,
    )
    operands = tuple(pltpu.with_memory_space_constraint(x, pltpu.HBM) for x in operands)
    result, weight = pl.pallas_call(
        kernel,
        out_shape=(
            pltpu.VMEM((rows * lon, cols), BF16),
            pltpu.VMEM((channels, channels), F32),
        ),
        in_specs=[pl.BlockSpec(memory_space=pltpu.HBM)] * len(operands),
        out_specs=(pl.BlockSpec(memory_space=pltpu.VMEM),) * 2,
        scratch_shapes=[
            pltpu.VMEM((2, rows * lon, cols), BF16),
            pltpu.VMEM((chans, modes * degrees, 2, channels), BF16),
            pltpu.VMEM((members * chans, modes, held, degrees), BF16),
            pltpu.VMEM(mixing.shape, BF16),
            *[pltpu.VMEM(constant.shape, BF16) for constant in constants],
            pltpu.VMEM((members, 2, 3, channels // 2, lats // members * pad), BF16),
            pltpu.VMEM((lats, pad, LANES), BF16),
            pltpu.VMEM((chans * lats, pad, LANES), BF16),
            pltpu.VMEM((chans * lats, pad, LANES), BF16),
            pltpu.VMEM((lats, pad, LANES), BF16),
            pltpu.VMEM((pieces, piece, channels), BF16),
            pltpu.VMEM((2 * pieces, piece, channels), BF16),
            pltpu.VMEM((pieces, piece, channels), BF16),
            dma((5,)),
            dma((3,)),
            dma((2,)),
            dma((2,)),
            dma((4,)),
            dma((2 + lats,)),
            pltpu.SemaphoreType.REGULAR,
        ],
        compiler_params=pltpu.CompilerParams(
            collective_id=0, has_side_effects=True, vmem_limit_bytes=48 << 20
        ),
    )(*operands)
    result, weight = stored_whole(result, weight)
    return result.reshape(grad_out.shape), weight


def fits(mesh, rows, lon, channels):
    lats, chans, members = (mesh.shape[axis] for axis in ("lat", "chan", "ens"))
    return (
        members == 2 and chans == 2 and lats == 4 and rows * lon <= 512
        and lon % 16 == 0 and rows % 2 == 0
        and channels // chans == LANES + LANES // 2
        and channels % (members * lats * 16) == 0
    )


def solution(mesh):
    placed = (
        P(("grp", "ens"), "lat", None, "chan"),
        P(("grp", "ens"), "lat", None, "chan"),
        P(("grp", "ens"), ("lat", "chan"), None, None, None),
        P(("lat", "chan"), None, "ens"),
        P(),
    )

    def local(grad_out, *rest):
        rows, lon, cols = grad_out.shape[1:]
        small = fits(mesh, rows, lon, cols * mesh.shape["chan"])
        return (fused if small else on_device)(grad_out, *rest)

    return jax.shard_map(
        local,
        mesh=mesh,
        in_specs=placed,
        out_specs=(P(("grp", "ens"), "lat", None, "chan"), P("grp", None)),
        check_vma=False,
    )
```

```python
import math

import jax
import jax.numpy as jnp
import numpy as np
from jax import lax
from jax.experimental import pallas as pl
from jax.experimental.pallas import tpu as pltpu
from jax.sharding import PartitionSpec as P


def fourier_table(lon_count, mode_count):
    longitude = jnp.arange(lon_count, dtype=jnp.int32)[:, None]
    wavenumber = jnp.arange(mode_count, dtype=jnp.int32)[None, :]
    product_index = longitude * wavenumber % lon_count
    angles = 2.0 * math.pi / lon_count * product_index.astype(jnp.float32)
    factor = math.sqrt(2.0 / lon_count)
    stacked = jnp.stack([jnp.cos(angles), -jnp.sin(angles)], axis=2) * factor
    return stacked.reshape(lon_count, 2 * mode_count).astype(jnp.bfloat16)


def silu_backward(cotangent, preact):
    values = preact.astype(jnp.float32)
    gate_value = jax.nn.sigmoid(values)
    return (
        cotangent.astype(jnp.float32) * gate_value * (1.0 + values * (1.0 - gate_value))
    ).astype(jnp.bfloat16)


def on_device(grad_out, pre_act, coeffs, legendre, mixing):
    lat_rows = grad_out.shape[1]
    lon_count = grad_out.shape[2]
    chan_cols = grad_out.shape[3]
    mode_count = lon_count // 2
    lat_devices = lax.axis_size("lat")
    chan_count = lax.axis_size("chan")
    members = lax.axis_size("ens")
    lat_count = lat_rows * lat_devices
    channels = chan_cols * chan_count
    mode_width = 2 * mode_count // (lat_devices * chan_count)
    local_modes = mode_width // 2
    fourier = fourier_table(lon_count, mode_count)
    scaled = silu_backward(grad_out[0], pre_act[0])
    spectral = jnp.einsum(
        "nk,anc->akc", fourier, scaled, preferred_element_type=jnp.float32
    ).astype(jnp.bfloat16)
    exchanged = lax.all_to_all(
        lax.all_to_all(spectral, "lat", split_axis=1, concat_axis=0, tiled=True),
        "chan",
        split_axis=1,
        concat_axis=2,
        tiled=True,
    )
    spectral_modes = exchanged.reshape(lat_count, local_modes, 2, channels)
    legendre_full = lax.all_gather(legendre, "ens", axis=2, tiled=True)
    coef_grad = jnp.einsum(
        "mla,amrc->mlrc", legendre_full, spectral_modes, preferred_element_type=jnp.float32
    ).astype(jnp.bfloat16)
    stored = coeffs[0].reshape(-1, channels)
    flat_grad = coef_grad.reshape(-1, channels)
    weight_grad = lax.dot_general(
        stored, flat_grad, (((0,), (0,)), ((), ())), preferred_element_type=jnp.float32
    )
    weight_grad = weight_grad * (1.0 / (members * mode_count))
    weight_grad = lax.psum(weight_grad, ("lat", "chan", "ens"))
    mixed_grad = lax.dot_general(
        coef_grad, mixing, (((3,), (1,)), ((), ())), preferred_element_type=jnp.float32
    ).astype(jnp.bfloat16)
    returned = jnp.einsum(
        "mla,mlrc->amrc", legendre_full, mixed_grad, preferred_element_type=jnp.float32
    ).astype(jnp.bfloat16)
    shaped = returned.reshape(lat_count, 1, mode_width, channels)
    received = lax.all_to_all(
        lax.all_to_all(shaped, "lat", split_axis=0, concat_axis=1, tiled=True),
        "chan",
        split_axis=3,
        concat_axis=2,
        tiled=True,
    )
    row_coeffs = received.reshape(lat_rows, 2 * mode_count, chan_cols)
    spatial = jnp.einsum("nk,akc->anc", fourier, row_coeffs, preferred_element_type=jnp.float32)
    result = (grad_out[0].astype(jnp.float32) + spatial).astype(jnp.bfloat16)
    return (result[None], weight_grad)

MESH = pl.DeviceIdType.MESH
BF16 = jnp.bfloat16
F32 = jnp.float32


def dot(a, b, dims=((1,), (0,))):
    return lax.dot_general(a, b, (dims, ((), ())), preferred_element_type=F32)


LANES = 128


def slots(rows, width):
    whole = [(a, a, k) for a in range(rows) for k in range(width)]
    paired = [(a, a + 1, k) for a in range(0, rows, 2) for k in range(width)]
    return whole, paired


def padded(rows, width):
    return -(-(rows + rows // 2) * width // 16) * 16


def tables(rows, lon, lats, chans, members, modes, degrees):
    width = 2 * modes * chans
    pad = padded(rows, width)
    n = np.arange(lon)[:, None]
    m = np.arange(lon // 2)[None, :]
    angles = np.float32(2.0 * math.pi / lon) * (n * m % lon).astype(np.float32)
    table = np.stack([np.cos(angles), -np.sin(angles)], axis=2).reshape(lon, lon)
    table = (table * np.float32(math.sqrt(2.0 / lon))).astype(np.float32)
    groups = rows + rows // 2
    inverse = np.zeros((groups, lon, lats, pad), np.float32)
    for g in range(groups):
        for d in range(lats):
            inverse[g, :, d, g * width:(g + 1) * width] = table[:, d * width:(d + 1) * width]
    inverse = inverse.reshape(groups * lon, lats * pad)
    whole, paired = slots(rows, width)
    near = lats // members
    lat_of = np.full((3, near, pad), -1)
    key_of = np.full((near, pad), -1)
    for z in range(near):
        for i, (even, odd, k) in enumerate(whole + paired):
            key_of[z, i] = k
            kinds = ((0, even),) if i < len(whole) else ((1, even), (2, odd))
            for kind, lat in kinds:
                lat_of[kind, z, i] = z * rows + lat
    lat_of, key_of = lat_of.reshape(3, -1), key_of.reshape(-1)
    select = (lat_of[:, None, :] == np.arange(near * rows)[None, :, None]).astype(np.float32)
    row = np.arange(chans * modes * degrees * 2)
    spread = (np.arange(chans * modes * degrees)[:, None] == row[None, :] // 2).astype(np.float32)
    row_key = row // (2 * degrees) * 2 + row % 2
    mask = (row_key[:, None] == key_of[None, :]).astype(np.float32)
    width = lats * pad
    tables = [mask, mask.T, spread]
    tables += [np.pad(part, ((0, -part.shape[0] % 16), (0, 0))) for part in select]
    tables = [np.pad(part, ((0, 0), (0, width - part.shape[1]))) for part in tables + [inverse]]
    starts = np.cumsum([0] + [part.shape[0] for part in tables]).tolist()
    cast = lambda x: jnp.asarray(np.ascontiguousarray(x), BF16)
    return cast(inverse.T), cast(np.concatenate(tables, axis=0)), starts


def swap_halves(x):
    return pltpu.roll(x, LANES // 2, 1)


def lower_half(x):
    return lax.broadcasted_iota(jnp.int32, x.shape, 1) < LANES // 2


def joined(wide, even, odd):
    first, second = wide[:, :LANES], wide[:, LANES:]
    low = lower_half(first)
    none = jnp.zeros_like(first)
    middle = jnp.where(low, even[:, :LANES], none)
    middle = middle + swap_halves(jnp.where(low, second, odd[:, :LANES]))
    last = jnp.where(low, none, odd[:, LANES:])
    last = last + swap_halves(jnp.where(low, even[:, LANES:], second))
    return jnp.concatenate([first, middle, last], axis=1).astype(BF16)


def parted(wide, even, odd):
    low = lower_half(even[:, :LANES])
    rest = jnp.where(low, even[:, :LANES], odd[:, LANES:])
    rest = rest + swap_halves(jnp.where(low, even[:, LANES:], odd[:, :LANES]))
    return jnp.concatenate([wide, rest], axis=1).astype(BF16)


def in_order(parts):
    first, second, rest = (parts[:, i * LANES:(i + 1) * LANES] for i in range(3))
    low, second = lower_half(first), swap_halves(second)
    return jnp.concatenate(
        [first, jnp.where(low, rest, second), jnp.where(low, second, rest)], axis=1
    )


def fused_kernel(
    lats, chans, members, lon, starts,
    grad_hbm, pre_hbm, coeffs_hbm, leg_hbm, mix_hbm, fwd_hbm, table_hbm,
    out_ref, weight_ref,
    point_ref, coeffs_ref, lbuf, mix_ref, fwd_ref, table_ref,
    terms, sbuf, rbuf, sbuf2, rbuf2, w1s, w1r, full_ref,
    isem, lsem, esem, ssem, rsem, gsem, go,
):
    z, c, x = lax.axis_index("lat"), lax.axis_index("chan"), lax.axis_index("ens")
    pad = rbuf.shape[1]
    half = lats // 2
    high = z // half
    other = lax.rem(x + 1, members)
    sibling = {"chan": 1 - c}
    mine = z * members + x
    pieces, piece = full_ref.shape[:2]
    modes, held, degrees = lbuf.shape[1:]
    points = point_ref.shape[1]
    last = pieces - 1
    double = last - members

    def home(q):
        return q - q // last * members

    count, near = 2 * chans * modes * degrees, half * pad
    early_first = sorted(
        ((a, b) for a in range(lats) for b in range(members)), key=lambda place: (sum(place), place)
    )

    def table(index, rows, cols):
        return table_ref[starts[index]:starts[index] + rows, :cols]

    def remote(src, dst, send, recv, target):
        return pltpu.make_async_remote_copy(
            src_ref=src, dst_ref=dst, send_sem=send, recv_sem=recv,
            device_id=target, device_id_type=MESH,
        )

    def done(ref, sem):
        pltpu.make_async_copy(ref, ref, sem).wait()

    far_first = [high * j + (1 - high) * (lats - 1 - j) for j in range(half)]
    far_first += [high * half + lax.rem(z + j, half) for j in range(1, half)]
    near_first = [z] + far_first[::-1]
    order = [(pz, px) for pz in near_first for px in (x, other)][1:]

    def load(source, target, index):
        return pltpu.make_async_copy(source, target, isem.at[index])

    urgent = load(fwd_hbm, fwd_ref, 1)
    shared = [load(leg_hbm, lbuf.at[x * chans + c], 2), load(table_hbm, table_ref, 3)]
    own_coeffs = load(coeffs_hbm, coeffs_ref.at[1], 4)
    own_mix = load(mix_hbm, mix_ref, 4)
    load(pre_hbm, point_ref.at[0], 0).start()
    load(grad_hbm, point_ref.at[1], 0).start()
    quarter = fwd_ref.shape[0] // lats
    for i in range(lats):
        rows = pl.ds(i * quarter, quarter)
        load(fwd_hbm.at[rows], fwd_ref.at[rows], 1).start()

    barrier = pltpu.get_barrier_semaphore()

    def announce(**target):
        pl.semaphore_signal(barrier, inc=1, device_id=target, device_id_type=MESH)

    @pl.when(c == 1)
    def _():
        for pz in far_first:
            for pc in (0, 1):
                announce(lat=pz, chan=pc)

    announce(ens=other, chan=c)
    announce(ens=other, chan=1 - c)
    announce(chan=1 - c)

    for copy in shared:
        copy.start()

    @pl.when(c == 0)
    def _():
        own_mix.start()

    @pl.when(c == 1)
    def _():
        own_coeffs.start()

    done(point_ref, isem.at[0])
    values = point_ref[0].astype(F32)
    gate = jax.nn.sigmoid(values)
    scaled = point_ref[1].astype(F32) * gate * (1.0 + values * (1.0 - gate))
    tail = scaled[:, LANES:].reshape(-1, 2, lon, LANES // 2)
    paired = jnp.concatenate([tail[:, 0], tail[:, 1]], axis=-1).reshape(-1, LANES)
    packed = jnp.concatenate([scaled[:, :LANES], paired], axis=0).astype(BF16)
    urgent.wait()
    sbuf[...] = dot(fwd_ref[...], packed).astype(BF16).reshape(lats, pad, LANES)

    pl.semaphore_wait(barrier, lats + members * chans - 2)

    leg = x * chans + c
    for px, pc, kind in ((other, c, 1), (other, 1 - c, 1), (x, 1 - c, 0)):
        remote(
            leg_hbm, lbuf.at[leg], isem.at[1], lsem.at[kind], {"ens": px, "chan": pc}
        ).start()
    for q in far_first:
        remote(
            sbuf.at[q], rbuf.at[c * lats + z], isem.at[0], esem.at[0], {"lat": q, "chan": 1}
        ).start()

    def transform(px):
        row = [lbuf[px * chans + pc, m].astype(F32) for pc in range(chans) for m in range(modes)]
        spread = table(2, count // 2, count)
        maps = dot(jnp.concatenate(row, axis=1).astype(BF16), spread).astype(BF16)
        down = ((0,), (0,))
        analysis = [
            dot(maps, table(3 + v, held, near), down).astype(BF16) * table(0, count, near)
            for v in range(3)
        ]
        return maps, analysis

    def maps_here():
        for copy in shared:
            copy.wait()
        done(lbuf.at[x * chans + 1 - c], lsem.at[0])

    def maps_there():
        done(lbuf.at[pl.ds(other * chans, chans)], lsem.at[1])

    def received(px):
        return jnp.concatenate(
            [rbuf[pl.ds(h * lats + px * half, half)].reshape(-1, LANES) for h in range(chans)],
            axis=1,
        )

    def back_to_grid():
        inverse = table(6, points + points // 2, lats * pad)
        spatial = dot(inverse, rbuf2[...].reshape(lats * pad, LANES))
        pairs = spatial[points:].reshape(-1, 1, lon, LANES)
        low, up = pairs[..., :LANES // 2], pairs[..., LANES // 2:]
        rest = jnp.concatenate([low, up], axis=1).reshape(points, LANES // 2)
        spatial = jnp.concatenate([spatial[:points], rest], axis=1)
        out_ref[...] = (point_ref[1].astype(F32) + spatial).astype(BF16)

    mean = 1.0 / (members * lon // 2)

    def average(pz):
        start = pz * members * piece
        rows = pl.ds(pl.multiple_of(start, members * piece), members * piece)
        value = full_ref[pl.ds(pz * members, members)].astype(F32) * mean
        weight_ref[rows, :] = in_order(value.reshape(members * piece, value.shape[2]))

    @pl.when(c == 0)
    def _():
        passed = remote(coeffs_hbm, coeffs_ref.at[0], ssem.at[0], ssem.at[1], sibling)
        passed.start()
        remote(
            sbuf.at[z], rbuf.at[c * lats + z], isem.at[0], esem.at[0], sibling
        ).start()
        maps_here()
        maps_there()
        own_mix.wait()
        analysis, synthesis = [], []
        for px in range(members):
            maps, down = transform(px)
            analysis.append(down)
            synthesis.append([
                dot(table(3 + v, held, near), maps, ((0,), (0,))).astype(BF16)
                * table(1, near, count)
                for v in range(3)
            ])
        done(rbuf, ssem.at[1])
        block = received(0), received(1)
        coef = joined(*(
            dot(analysis[0][v], block[0]) + dot(analysis[1][v], block[1]) for v in range(3)
        ))
        mixed = dot(coef, mix_ref[...], ((1,), (1,)))
        t0, t1, t2 = (mixed[:, i * LANES:(i + 1) * LANES] for i in range(3))
        low = lower_half(t0)
        none = jnp.zeros_like(t0)
        even0, odd1 = jnp.where(low, t1, none), jnp.where(low, none, t2)
        sides = (
            (t0, swap_halves(jnp.where(low, t2, t1))),
            (even0, swap_halves(odd1)),
            (swap_halves(even0), odd1),
        )
        sides = [jnp.concatenate(side, axis=1).astype(BF16) for side in sides]

        def send_home(q):
            for h in range(chans):
                remote(
                    sbuf2.at[h * lats + q], rbuf2.at[z], isem.at[2], rsem.at[1],
                    {"lat": q, "chan": h},
                ).start()

        for px in range(members):
            back = sum(dot(matrix, side) for matrix, side in zip(synthesis[px], sides)).astype(BF16)
            for h in range(chans):
                part = back[:, h * LANES:(h + 1) * LANES].reshape(half, pad, LANES)
                sbuf2[h * lats + px * half:h * lats + (px + 1) * half] = part
            if px == 0:
                pl.when(z > 0)(lambda: send_home(0))
            else:
                pl.when(z == 0)(lambda: send_home(lats - 1))
        pl.semaphore_wait(go, 1)
        for j in range(1, lats - 1):
            send_home(j + jnp.where(jnp.logical_and(z > 0, z <= j), 1, 0))
        remote(sbuf2.at[lats + z], rbuf2.at[z], isem.at[2], rsem.at[1], sibling).start()
        rbuf2[z] = sbuf2[z]
        passed.wait_send()
        done(sbuf, isem.at[0])
        done(lbuf.at[pl.ds(0, members * chans - 1)], isem.at[1])
        done(rbuf2.at[pl.ds(0, lats - 1)], rsem.at[1])
        back_to_grid()
        done(sbuf2.at[pl.ds(0, chans * lats - 1)], isem.at[2])
        for pz in near_first:
            done(full_ref.at[pl.ds(pz * members, members)], gsem.at[pz])
            average(pz)

    @pl.when(c == 1)
    def _():
        rbuf[lats + z] = sbuf[z]
        own_coeffs.wait()
        done(coeffs_ref.at[0], ssem.at[1])
        flat = coeffs_ref[...].reshape(-1, coeffs_ref.shape[-1])
        stored = flat.astype(F32).T.astype(BF16)
        maps_here()
        for px in (x, other):
            if px is other:
                maps_there()
            _, analysis = transform(px)
            for v in range(3):
                value = dot(stored, analysis[v]).astype(BF16)
                terms[px, :, v] = value.reshape(2, -1, value.shape[1])

        done(rbuf.at[pl.ds(0, chans * lats - 1)], esem.at[0])
        block = remote(rbuf, rbuf, ssem.at[0], ssem.at[1], sibling)
        block.start()
        arrays = received(0), received(1)
        for group, targets in ((1 - high, far_first[:half]), (high, far_first[half:] + [z])):
            value = parted(*(
                dot(terms[0, group, v], arrays[0]) + dot(terms[1, group, v], arrays[1])
                for v in range(3)
            ))
            share = half * members
            w1s[pl.ds(group * share, share)] = value.reshape(share, piece, value.shape[1])
            for pz in targets:
                for px in (other, x):
                    q = pz * members + px
                    copy = remote(
                        w1s.at[q], w1r.at[q // last * pieces + mine], isem.at[2],
                        rsem.at[2 * (q // last)], {"lat": home(q) // members, "ens": px},
                    )
                    pl.when(home(q) != mine)(copy.start)

        @pl.when(mine == last)
        def _():
            done(w1s, isem.at[2])

        @pl.when(mine == double)
        def _():
            done(w1s.at[pl.ds(0, pieces - 2)], isem.at[2])

        @pl.when(jnp.logical_and(mine != last, mine != double))
        def _():
            done(w1s.at[pl.ds(0, pieces - 1)], isem.at[2])

        pl.semaphore_signal(go, inc=1, device_id=sibling, device_id_type=MESH)

        block.wait_send()
        done(sbuf.at[pl.ds(0, lats - 1)], isem.at[0])
        done(lbuf.at[pl.ds(0, members * chans - 1)], isem.at[1])

        def reduced(slot, index):
            start = slot * pieces
            done(w1r.at[pl.ds(start, pieces - 1)], rsem.at[2 * slot])
            total = w1s[index].astype(F32)
            for pz, px in order:
                total = total + w1r[start + pz * members + px].astype(F32)
            full_ref[index] = total.astype(BF16)

        @pl.when(mine != last)
        def _():
            reduced(0, mine)

        @pl.when(mine == double)
        def _():
            reduced(1, last)

        for pz, px in early_first:
            target = {"lat": pz, "ens": px}
            away = pz * members + px != mine
            first = remote(
                full_ref.at[mine], full_ref.at[mine], isem.at[4], gsem.at[z], target
            )
            second = remote(
                full_ref.at[last], full_ref.at[last], isem.at[4], gsem.at[lats - 1], target
            )
            pl.when(jnp.logical_and(away, mine != last))(first.start)
            pl.when(jnp.logical_and(away, mine == double))(second.start)
        for pz in near_first:
            both = full_ref.at[pl.ds(pz * members, members)]
            one = full_ref.at[pz * members + other]
            if pz is z:
                single = mine != last
            else:
                single = jnp.logical_and(mine == double, pz == lats - 1)

            @pl.when(single)
            def _():
                done(one, gsem.at[pz])

            @pl.when(jnp.logical_not(single))
            def _():
                done(both, gsem.at[pz])

            remote(both, both, isem.at[3], gsem.at[pz], sibling).start()
            average(pz)
        done(rbuf2, rsem.at[1])
        back_to_grid()

        @pl.when(mine == double)
        def _():
            done(w1r.at[pl.ds(0, 2 * pieces - 2)], isem.at[4])

        @pl.when(jnp.logical_and(mine != last, mine != double))
        def _():
            done(full_ref.at[pl.ds(0, pieces - 1)], isem.at[4])

        done(full_ref, isem.at[3])


def store_kernel(result, weight, result_hbm, weight_hbm, sems):
    stores = [
        pltpu.make_async_copy(weight, weight_hbm, sems.at[0]),
        pltpu.make_async_copy(result, result_hbm, sems.at[1]),
    ]
    for store in stores:
        store.start()
    for store in stores:
        store.wait()


def stored_whole(result, weight):
    return pl.pallas_call(
        store_kernel,
        out_shape=tuple(jax.ShapeDtypeStruct(x.shape, x.dtype) for x in (result, weight)),
        in_specs=[pl.BlockSpec(memory_space=pl.ANY)] * 2,
        out_specs=(pl.BlockSpec(memory_space=pltpu.HBM),) * 2,
        scratch_shapes=[pltpu.SemaphoreType.DMA((2,))],
        compiler_params=pltpu.CompilerParams(vmem_limit_bytes=1 << 20),
    )(result, weight)


def fused(grad_out, pre_act, coeffs, legendre, mixing):
    rows, lon, cols = grad_out.shape[1:]
    lats, chans = lax.axis_size("lat"), lax.axis_size("chan")
    members = lax.axis_size("ens")
    modes, degrees, held = legendre.shape
    channels = cols * chans
    pad = padded(rows, 2 * modes * chans)
    pieces = lats * members
    piece = channels // pieces
    *constants, starts = tables(rows, lon, lats, chans, members, modes, degrees)
    dma = pltpu.SemaphoreType.DMA

    def kernel(*refs):
        fused_kernel(lats, chans, members, lon, starts, *refs)

    operands = (
        grad_out.reshape(rows * lon, cols),
        pre_act.reshape(rows * lon, cols),
        coeffs.reshape(modes * degrees, 2, channels),
        legendre.transpose(0, 2, 1),
        mixing,
        *constants,
    )
    operands = tuple(pltpu.with_memory_space_constraint(x, pltpu.HBM) for x in operands)
    result, weight = pl.pallas_call(
        kernel,
        out_shape=(
            pltpu.VMEM((rows * lon, cols), BF16),
            pltpu.VMEM((channels, channels), F32),
        ),
        in_specs=[pl.BlockSpec(memory_space=pltpu.HBM)] * len(operands),
        out_specs=(pl.BlockSpec(memory_space=pltpu.VMEM),) * 2,
        scratch_shapes=[
            pltpu.VMEM((2, rows * lon, cols), BF16),
            pltpu.VMEM((chans, modes * degrees, 2, channels), BF16),
            pltpu.VMEM((members * chans, modes, held, degrees), BF16),
            pltpu.VMEM(mixing.shape, BF16),
            *[pltpu.VMEM(constant.shape, BF16) for constant in constants],
            pltpu.VMEM((members, 2, 3, channels // 2, lats // members * pad), BF16),
            pltpu.VMEM((lats, pad, LANES), BF16),
            pltpu.VMEM((chans * lats, pad, LANES), BF16),
            pltpu.VMEM((chans * lats, pad, LANES), BF16),
            pltpu.VMEM((lats, pad, LANES), BF16),
            pltpu.VMEM((pieces, piece, channels), BF16),
            pltpu.VMEM((2 * pieces, piece, channels), BF16),
            pltpu.VMEM((pieces, piece, channels), BF16),
            dma((5,)),
            dma((2,)),
            dma((1,)),
            dma((2,)),
            dma((3,)),
            dma((lats,)),
            pltpu.SemaphoreType.REGULAR,
        ],
        compiler_params=pltpu.CompilerParams(
            collective_id=0, has_side_effects=True, vmem_limit_bytes=48 << 20
        ),
    )(*operands)
    result, weight = stored_whole(result, weight)
    return result.reshape(grad_out.shape), weight


def fits(mesh, rows, lon, channels):
    lats, chans, members = (mesh.shape[axis] for axis in ("lat", "chan", "ens"))
    return (
        members == 2 and chans == 2 and lats == 4 and rows * lon <= 512
        and lon % 16 == 0 and rows % 2 == 0
        and channels // chans == LANES + LANES // 2
        and channels % (members * lats * 16) == 0
    )


def solution(mesh):
    placed = (
        P(("grp", "ens"), "lat", None, "chan"),
        P(("grp", "ens"), "lat", None, "chan"),
        P(("grp", "ens"), ("lat", "chan"), None, None, None),
        P(("lat", "chan"), None, "ens"),
        P(),
    )

    def local(grad_out, *rest):
        rows, lon, cols = grad_out.shape[1:]
        small = fits(mesh, rows, lon, cols * mesh.shape["chan"])
        return (fused if small else on_device)(grad_out, *rest)

    return jax.shard_map(
        local,
        mesh=mesh,
        in_specs=placed,
        out_specs=(P(("grp", "ens"), "lat", None, "chan"), P("grp", None)),
        check_vma=False,
    )
```

```python
import math

import jax
import jax.numpy as jnp
import numpy as np
from jax import lax
from jax.experimental import pallas as pl
from jax.experimental.pallas import tpu as pltpu
from jax.sharding import PartitionSpec as P


def fourier_table(lon_count, mode_count):
    longitude = jnp.arange(lon_count, dtype=jnp.int32)[:, None]
    wavenumber = jnp.arange(mode_count, dtype=jnp.int32)[None, :]
    product_index = longitude * wavenumber % lon_count
    angles = 2.0 * math.pi / lon_count * product_index.astype(jnp.float32)
    factor = math.sqrt(2.0 / lon_count)
    stacked = jnp.stack([jnp.cos(angles), -jnp.sin(angles)], axis=2) * factor
    return stacked.reshape(lon_count, 2 * mode_count).astype(jnp.bfloat16)


def silu_backward(cotangent, preact):
    values = preact.astype(jnp.float32)
    gate_value = jax.nn.sigmoid(values)
    return (
        cotangent.astype(jnp.float32) * gate_value * (1.0 + values * (1.0 - gate_value))
    ).astype(jnp.bfloat16)


def on_device(grad_out, pre_act, coeffs, legendre, mixing):
    lat_rows = grad_out.shape[1]
    lon_count = grad_out.shape[2]
    chan_cols = grad_out.shape[3]
    mode_count = lon_count // 2
    lat_devices = lax.axis_size("lat")
    chan_count = lax.axis_size("chan")
    members = lax.axis_size("ens")
    lat_count = lat_rows * lat_devices
    channels = chan_cols * chan_count
    mode_width = 2 * mode_count // (lat_devices * chan_count)
    local_modes = mode_width // 2
    fourier = fourier_table(lon_count, mode_count)
    scaled = silu_backward(grad_out[0], pre_act[0])
    spectral = jnp.einsum(
        "nk,anc->akc", fourier, scaled, preferred_element_type=jnp.float32
    ).astype(jnp.bfloat16)
    exchanged = lax.all_to_all(
        lax.all_to_all(spectral, "lat", split_axis=1, concat_axis=0, tiled=True),
        "chan",
        split_axis=1,
        concat_axis=2,
        tiled=True,
    )
    spectral_modes = exchanged.reshape(lat_count, local_modes, 2, channels)
    legendre_full = lax.all_gather(legendre, "ens", axis=2, tiled=True)
    coef_grad = jnp.einsum(
        "mla,amrc->mlrc", legendre_full, spectral_modes, preferred_element_type=jnp.float32
    ).astype(jnp.bfloat16)
    stored = coeffs[0].reshape(-1, channels)
    flat_grad = coef_grad.reshape(-1, channels)
    weight_grad = lax.dot_general(
        stored, flat_grad, (((0,), (0,)), ((), ())), preferred_element_type=jnp.float32
    )
    weight_grad = weight_grad * (1.0 / (members * mode_count))
    weight_grad = lax.psum(weight_grad, ("lat", "chan", "ens"))
    mixed_grad = lax.dot_general(
        coef_grad, mixing, (((3,), (1,)), ((), ())), preferred_element_type=jnp.float32
    ).astype(jnp.bfloat16)
    returned = jnp.einsum(
        "mla,mlrc->amrc", legendre_full, mixed_grad, preferred_element_type=jnp.float32
    ).astype(jnp.bfloat16)
    shaped = returned.reshape(lat_count, 1, mode_width, channels)
    received = lax.all_to_all(
        lax.all_to_all(shaped, "lat", split_axis=0, concat_axis=1, tiled=True),
        "chan",
        split_axis=3,
        concat_axis=2,
        tiled=True,
    )
    row_coeffs = received.reshape(lat_rows, 2 * mode_count, chan_cols)
    spatial = jnp.einsum("nk,akc->anc", fourier, row_coeffs, preferred_element_type=jnp.float32)
    result = (grad_out[0].astype(jnp.float32) + spatial).astype(jnp.bfloat16)
    return (result[None], weight_grad)

MESH = pl.DeviceIdType.MESH
BF16 = jnp.bfloat16
F32 = jnp.float32


def dot(a, b, dims=((1,), (0,))):
    return lax.dot_general(a, b, (dims, ((), ())), preferred_element_type=F32)


LANES = 128


def slots(rows, width):
    whole = [(a, a, k) for a in range(rows) for k in range(width)]
    paired = [(a, a + 1, k) for a in range(0, rows, 2) for k in range(width)]
    return whole, paired


def padded(rows, width):
    return -(-(rows + rows // 2) * width // 16) * 16


def tables(rows, lon, lats, chans, members, modes, degrees):
    width = 2 * modes * chans
    pad = padded(rows, width)
    n = np.arange(lon)[:, None]
    m = np.arange(lon // 2)[None, :]
    angles = np.float32(2.0 * math.pi / lon) * (n * m % lon).astype(np.float32)
    table = np.stack([np.cos(angles), -np.sin(angles)], axis=2).reshape(lon, lon)
    table = (table * np.float32(math.sqrt(2.0 / lon))).astype(np.float32)
    groups = rows + rows // 2
    inverse = np.zeros((groups, lon, lats, pad), np.float32)
    for g in range(groups):
        for d in range(lats):
            inverse[g, :, d, g * width:(g + 1) * width] = table[:, d * width:(d + 1) * width]
    inverse = inverse.reshape(groups * lon, lats * pad)
    whole, paired = slots(rows, width)
    near = lats // members
    lat_of = np.full((3, near, pad), -1)
    key_of = np.full((near, pad), -1)
    for z in range(near):
        for i, (even, odd, k) in enumerate(whole + paired):
            key_of[z, i] = k
            kinds = ((0, even),) if i < len(whole) else ((1, even), (2, odd))
            for kind, lat in kinds:
                lat_of[kind, z, i] = z * rows + lat
    lat_of, key_of = lat_of.reshape(3, -1), key_of.reshape(-1)
    select = (lat_of[:, None, :] == np.arange(near * rows)[None, :, None]).astype(np.float32)
    row = np.arange(chans * modes * degrees * 2)
    spread = (np.arange(chans * modes * degrees)[:, None] == row[None, :] // 2).astype(np.float32)
    row_key = row // (2 * degrees) * 2 + row % 2
    mask = (row_key[:, None] == key_of[None, :]).astype(np.float32)
    width = lats * pad
    tables = [mask, mask.T, spread]
    tables += [np.pad(part, ((0, -part.shape[0] % 16), (0, 0))) for part in select]
    tables = [np.pad(part, ((0, 0), (0, width - part.shape[1]))) for part in tables + [inverse]]
    starts = np.cumsum([0] + [part.shape[0] for part in tables]).tolist()
    cast = lambda x: jnp.asarray(np.ascontiguousarray(x), BF16)
    return cast(inverse.T), cast(np.concatenate(tables, axis=0)), starts


def swap_halves(x):
    return pltpu.roll(x, LANES // 2, 1)


def lower_half(x):
    return lax.broadcasted_iota(jnp.int32, x.shape, 1) < LANES // 2


def joined(wide, even, odd):
    first, second = wide[:, :LANES], wide[:, LANES:]
    low = lower_half(first)
    none = jnp.zeros_like(first)
    middle = jnp.where(low, even[:, :LANES], none)
    middle = middle + swap_halves(jnp.where(low, second, odd[:, :LANES]))
    last = jnp.where(low, none, odd[:, LANES:])
    last = last + swap_halves(jnp.where(low, even[:, LANES:], second))
    return jnp.concatenate([first, middle, last], axis=1).astype(BF16)


def parted(wide, even, odd):
    low = lower_half(even[:, :LANES])
    rest = jnp.where(low, even[:, :LANES], odd[:, LANES:])
    rest = rest + swap_halves(jnp.where(low, even[:, LANES:], odd[:, :LANES]))
    return jnp.concatenate([wide, rest], axis=1).astype(BF16)


def in_order(parts):
    first, second, rest = (parts[:, i * LANES:(i + 1) * LANES] for i in range(3))
    low, second = lower_half(first), swap_halves(second)
    return jnp.concatenate(
        [first, jnp.where(low, rest, second), jnp.where(low, second, rest)], axis=1
    )


def fused_kernel(
    lats, chans, members, lon, starts,
    grad_hbm, pre_hbm, coeffs_hbm, leg_hbm, mix_hbm, fwd_hbm, table_hbm,
    out_ref, weight_ref,
    point_ref, coeffs_ref, lbuf, mix_ref, fwd_ref, table_ref,
    terms, sbuf, rbuf, sbuf2, rbuf2, w1s, w1r, full_ref,
    isem, lsem, esem, ssem, rsem, gsem, go,
):
    z, c, x = lax.axis_index("lat"), lax.axis_index("chan"), lax.axis_index("ens")
    pad = rbuf.shape[1]
    half = lats // 2
    high = z // half
    other = lax.rem(x + 1, members)
    sibling = {"chan": 1 - c}
    mine = z * members + x
    pieces, piece = full_ref.shape[:2]
    modes, held, degrees = lbuf.shape[1:]
    points = point_ref.shape[1]
    last = pieces - 1
    double = last - members

    def home(q):
        return q - q // last * members

    count, near = 2 * chans * modes * degrees, half * pad
    early_first = sorted(
        ((a, b) for a in range(lats) for b in range(members)), key=lambda place: (sum(place), place)
    )

    def table(index, rows, cols):
        return table_ref[starts[index]:starts[index] + rows, :cols]

    def remote(src, dst, send, recv, target):
        return pltpu.make_async_remote_copy(
            src_ref=src, dst_ref=dst, send_sem=send, recv_sem=recv,
            device_id=target, device_id_type=MESH,
        )

    def done(ref, sem):
        pltpu.make_async_copy(ref, ref, sem).wait()

    far_first = [high * j + (1 - high) * (lats - 1 - j) for j in range(half)]
    far_first += [high * half + lax.rem(z + j, half) for j in range(1, half)]
    near_first = [z] + far_first[::-1]
    order = [(pz, px) for pz in near_first for px in (x, other)][1:]

    def load(source, target, index):
        return pltpu.make_async_copy(source, target, isem.at[index])

    urgent = load(fwd_hbm, fwd_ref, 1)
    shared = [load(leg_hbm, lbuf.at[x * chans + c], 2), load(table_hbm, table_ref, 3)]
    own_coeffs = load(coeffs_hbm, coeffs_ref.at[1], 4)
    own_mix = load(mix_hbm, mix_ref, 4)
    load(pre_hbm, point_ref.at[0], 0).start()
    load(grad_hbm, point_ref.at[1], 0).start()
    quarter = fwd_ref.shape[0] // lats
    for i in range(lats):
        rows = pl.ds(i * quarter, quarter)
        load(fwd_hbm.at[rows], fwd_ref.at[rows], 1).start()

    barrier = pltpu.get_barrier_semaphore()

    def announce(**target):
        pl.semaphore_signal(barrier, inc=1, device_id=target, device_id_type=MESH)

    @pl.when(c == 1)
    def _():
        for pz in far_first:
            for pc in (0, 1):
                announce(lat=pz, chan=pc)

    announce(ens=other, chan=c)
    announce(ens=other, chan=1 - c)
    announce(chan=1 - c)

    for copy in shared:
        copy.start()

    @pl.when(c == 0)
    def _():
        own_mix.start()

    @pl.when(c == 1)
    def _():
        own_coeffs.start()

    done(point_ref, isem.at[0])
    values = point_ref[0].astype(F32)
    gate = jax.nn.sigmoid(values)
    scaled = point_ref[1].astype(F32) * gate * (1.0 + values * (1.0 - gate))
    tail = scaled[:, LANES:].reshape(-1, 2, lon, LANES // 2)
    paired = jnp.concatenate([tail[:, 0], tail[:, 1]], axis=-1).reshape(-1, LANES)
    packed = jnp.concatenate([scaled[:, :LANES], paired], axis=0).astype(BF16)
    urgent.wait()
    sbuf[...] = dot(fwd_ref[...], packed).astype(BF16).reshape(lats, pad, LANES)

    pl.semaphore_wait(barrier, lats + members * chans - 2)

    leg = x * chans + c
    for px, pc, kind in ((other, c, 1), (other, 1 - c, 1), (x, 1 - c, 0)):
        remote(
            leg_hbm, lbuf.at[leg], isem.at[1], lsem.at[kind], {"ens": px, "chan": pc}
        ).start()
    for q in far_first:
        remote(
            sbuf.at[q], rbuf.at[c * lats + z], isem.at[0], esem.at[0], {"lat": q, "chan": 1}
        ).start()

    def transform(px):
        row = [lbuf[px * chans + pc, m].astype(F32) for pc in range(chans) for m in range(modes)]
        spread = table(2, count // 2, count)
        maps = dot(jnp.concatenate(row, axis=1).astype(BF16), spread).astype(BF16)
        down = ((0,), (0,))
        analysis = [
            dot(maps, table(3 + v, held, near), down).astype(BF16) * table(0, count, near)
            for v in range(3)
        ]
        return maps, analysis

    def maps_here():
        for copy in shared:
            copy.wait()
        done(lbuf.at[x * chans + 1 - c], lsem.at[0])

    def maps_there():
        done(lbuf.at[pl.ds(other * chans, chans)], lsem.at[1])

    def received(px):
        return jnp.concatenate(
            [rbuf[pl.ds(h * lats + px * half, half)].reshape(-1, LANES) for h in range(chans)],
            axis=1,
        )

    def back_to_grid():
        inverse = table(6, points + points // 2, lats * pad)
        spatial = dot(inverse, rbuf2[...].reshape(lats * pad, LANES))
        pairs = spatial[points:].reshape(-1, 1, lon, LANES)
        low, up = pairs[..., :LANES // 2], pairs[..., LANES // 2:]
        rest = jnp.concatenate([low, up], axis=1).reshape(points, LANES // 2)
        spatial = jnp.concatenate([spatial[:points], rest], axis=1)
        out_ref[...] = (point_ref[1].astype(F32) + spatial).astype(BF16)

    mean = 1.0 / (members * lon // 2)

    def average(pz):
        start = pz * members * piece
        rows = pl.ds(pl.multiple_of(start, members * piece), members * piece)
        value = full_ref[pl.ds(pz * members, members)].astype(F32) * mean
        weight_ref[rows, :] = in_order(value.reshape(members * piece, value.shape[2]))

    @pl.when(c == 0)
    def _():
        passed = remote(coeffs_hbm, coeffs_ref.at[0], ssem.at[0], ssem.at[1], sibling)
        passed.start()
        remote(
            sbuf.at[z], rbuf.at[c * lats + z], isem.at[0], esem.at[0], sibling
        ).start()
        maps_here()
        maps_there()
        own_mix.wait()
        analysis, synthesis = [], []
        for px in range(members):
            maps, down = transform(px)
            analysis.append(down)
            synthesis.append([
                dot(table(3 + v, held, near), maps, ((0,), (0,))).astype(BF16)
                * table(1, near, count)
                for v in range(3)
            ])
        done(rbuf, ssem.at[1])
        block = received(0), received(1)
        coef = joined(*(
            dot(analysis[0][v], block[0]) + dot(analysis[1][v], block[1]) for v in range(3)
        ))
        mixed = dot(coef, mix_ref[...], ((1,), (1,)))
        t0, t1, t2 = (mixed[:, i * LANES:(i + 1) * LANES] for i in range(3))
        low = lower_half(t0)
        none = jnp.zeros_like(t0)
        even0, odd1 = jnp.where(low, t1, none), jnp.where(low, none, t2)
        sides = (
            (t0, swap_halves(jnp.where(low, t2, t1))),
            (even0, swap_halves(odd1)),
            (swap_halves(even0), odd1),
        )
        sides = [jnp.concatenate(side, axis=1).astype(BF16) for side in sides]

        def send_home(q):
            for h in range(chans):
                remote(
                    sbuf2.at[h * lats + q], rbuf2.at[z], isem.at[2], rsem.at[1],
                    {"lat": q, "chan": h},
                ).start()

        for px in range(members):
            back = sum(dot(matrix, side) for matrix, side in zip(synthesis[px], sides)).astype(BF16)
            for h in range(chans):
                part = back[:, h * LANES:(h + 1) * LANES].reshape(half, pad, LANES)
                sbuf2[h * lats + px * half:h * lats + (px + 1) * half] = part
            if px == 0:
                pl.when(z > 0)(lambda: send_home(0))
            else:
                pl.when(z == 0)(lambda: send_home(lats - 1))
        pl.semaphore_wait(go, 1)
        for j in range(1, lats - 1):
            send_home(j + jnp.where(jnp.logical_and(z > 0, z <= j), 1, 0))
        remote(sbuf2.at[lats + z], rbuf2.at[z], isem.at[2], rsem.at[1], sibling).start()
        rbuf2[z] = sbuf2[z]
        passed.wait_send()
        done(sbuf, isem.at[0])
        done(lbuf.at[pl.ds(0, members * chans - 1)], isem.at[1])
        done(rbuf2.at[pl.ds(0, lats - 1)], rsem.at[1])
        back_to_grid()
        done(sbuf2.at[pl.ds(0, chans * lats - 1)], isem.at[2])
        for pz in near_first:
            done(full_ref.at[pl.ds(pz * members, members)], gsem.at[pz])
            average(pz)

    @pl.when(c == 1)
    def _():
        rbuf[lats + z] = sbuf[z]
        own_coeffs.wait()
        done(coeffs_ref.at[0], ssem.at[1])
        flat = coeffs_ref[...].reshape(-1, coeffs_ref.shape[-1])
        stored = flat.astype(F32).T.astype(BF16)
        maps_here()
        for px in (x, other):
            if px is other:
                maps_there()
            _, analysis = transform(px)
            for v in range(3):
                value = dot(stored, analysis[v]).astype(BF16)
                terms[px, :, v] = value.reshape(2, -1, value.shape[1])

        done(rbuf.at[pl.ds(0, chans * lats - 1)], esem.at[0])
        block = remote(rbuf, rbuf, ssem.at[0], ssem.at[1], sibling)
        block.start()
        arrays = received(0), received(1)
        for group, targets in ((1 - high, far_first[:half]), (high, far_first[half:] + [z])):
            value = parted(*(
                dot(terms[0, group, v], arrays[0]) + dot(terms[1, group, v], arrays[1])
                for v in range(3)
            ))
            share = half * members
            w1s[pl.ds(group * share, share)] = value.reshape(share, piece, value.shape[1])
            for pz in targets:
                for px in (other, x):
                    q = pz * members + px
                    copy = remote(
                        w1s.at[q], w1r.at[q // last * pieces + mine], isem.at[2],
                        rsem.at[2 * (q // last)], {"lat": home(q) // members, "ens": px},
                    )
                    pl.when(home(q) != mine)(copy.start)

        @pl.when(mine == last)
        def _():
            done(w1s, isem.at[2])

        @pl.when(mine == double)
        def _():
            done(w1s.at[pl.ds(0, pieces - 2)], isem.at[2])

        @pl.when(jnp.logical_and(mine != last, mine != double))
        def _():
            done(w1s.at[pl.ds(0, pieces - 1)], isem.at[2])

        pl.semaphore_signal(go, inc=1, device_id=sibling, device_id_type=MESH)

        block.wait_send()
        done(sbuf.at[pl.ds(0, lats - 1)], isem.at[0])
        done(lbuf.at[pl.ds(0, members * chans - 1)], isem.at[1])

        def reduced(slot, index):
            start = slot * pieces
            done(w1r.at[pl.ds(start, pieces - 1)], rsem.at[2 * slot])
            total = w1s[index].astype(F32)
            for pz, px in order:
                total = total + w1r[start + pz * members + px].astype(F32)
            full_ref[index] = total.astype(BF16)

        @pl.when(mine != last)
        def _():
            reduced(0, mine)

        @pl.when(mine == double)
        def _():
            reduced(1, last)

        for pz, px in early_first:
            target = {"lat": pz, "ens": px}
            away = pz * members + px != mine
            first = remote(
                full_ref.at[mine], full_ref.at[mine], isem.at[4], gsem.at[z], target
            )
            second = remote(
                full_ref.at[last], full_ref.at[last], isem.at[4], gsem.at[lats - 1], target
            )
            pl.when(jnp.logical_and(away, mine != last))(first.start)
            pl.when(jnp.logical_and(away, mine == double))(second.start)
        for pz in near_first:
            both = full_ref.at[pl.ds(pz * members, members)]
            one = full_ref.at[pz * members + other]
            if pz is z:
                single = mine != last
            else:
                single = jnp.logical_and(mine == double, pz == lats - 1)

            @pl.when(single)
            def _():
                done(one, gsem.at[pz])

            @pl.when(jnp.logical_not(single))
            def _():
                done(both, gsem.at[pz])

            remote(both, both, isem.at[3], gsem.at[pz], sibling).start()
        for pz in near_first:
            average(pz)
        done(rbuf2, rsem.at[1])
        back_to_grid()

        @pl.when(mine == double)
        def _():
            done(w1r.at[pl.ds(0, 2 * pieces - 2)], isem.at[4])

        @pl.when(jnp.logical_and(mine != last, mine != double))
        def _():
            done(full_ref.at[pl.ds(0, pieces - 1)], isem.at[4])

        done(full_ref, isem.at[3])


def store_kernel(result, weight, result_hbm, weight_hbm, sems):
    stores = [
        pltpu.make_async_copy(weight, weight_hbm, sems.at[0]),
        pltpu.make_async_copy(result, result_hbm, sems.at[1]),
    ]
    for store in stores:
        store.start()
    for store in stores:
        store.wait()


def stored_whole(result, weight):
    return pl.pallas_call(
        store_kernel,
        out_shape=tuple(jax.ShapeDtypeStruct(x.shape, x.dtype) for x in (result, weight)),
        in_specs=[pl.BlockSpec(memory_space=pl.ANY)] * 2,
        out_specs=(pl.BlockSpec(memory_space=pltpu.HBM),) * 2,
        scratch_shapes=[pltpu.SemaphoreType.DMA((2,))],
        compiler_params=pltpu.CompilerParams(vmem_limit_bytes=1 << 20),
    )(result, weight)


def fused(grad_out, pre_act, coeffs, legendre, mixing):
    rows, lon, cols = grad_out.shape[1:]
    lats, chans = lax.axis_size("lat"), lax.axis_size("chan")
    members = lax.axis_size("ens")
    modes, degrees, held = legendre.shape
    channels = cols * chans
    pad = padded(rows, 2 * modes * chans)
    pieces = lats * members
    piece = channels // pieces
    *constants, starts = tables(rows, lon, lats, chans, members, modes, degrees)
    dma = pltpu.SemaphoreType.DMA

    def kernel(*refs):
        fused_kernel(lats, chans, members, lon, starts, *refs)

    operands = (
        grad_out.reshape(rows * lon, cols),
        pre_act.reshape(rows * lon, cols),
        coeffs.reshape(modes * degrees, 2, channels),
        legendre.transpose(0, 2, 1),
        mixing,
        *constants,
    )
    operands = tuple(pltpu.with_memory_space_constraint(x, pltpu.HBM) for x in operands)
    result, weight = pl.pallas_call(
        kernel,
        out_shape=(
            pltpu.VMEM((rows * lon, cols), BF16),
            pltpu.VMEM((channels, channels), F32),
        ),
        in_specs=[pl.BlockSpec(memory_space=pltpu.HBM)] * len(operands),
        out_specs=(pl.BlockSpec(memory_space=pltpu.VMEM),) * 2,
        scratch_shapes=[
            pltpu.VMEM((2, rows * lon, cols), BF16),
            pltpu.VMEM((chans, modes * degrees, 2, channels), BF16),
            pltpu.VMEM((members * chans, modes, held, degrees), BF16),
            pltpu.VMEM(mixing.shape, BF16),
            *[pltpu.VMEM(constant.shape, BF16) for constant in constants],
            pltpu.VMEM((members, 2, 3, channels // 2, lats // members * pad), BF16),
            pltpu.VMEM((lats, pad, LANES), BF16),
            pltpu.VMEM((chans * lats, pad, LANES), BF16),
            pltpu.VMEM((chans * lats, pad, LANES), BF16),
            pltpu.VMEM((lats, pad, LANES), BF16),
            pltpu.VMEM((pieces, piece, channels), BF16),
            pltpu.VMEM((2 * pieces, piece, channels), BF16),
            pltpu.VMEM((pieces, piece, channels), BF16),
            dma((5,)),
            dma((2,)),
            dma((1,)),
            dma((2,)),
            dma((3,)),
            dma((lats,)),
            pltpu.SemaphoreType.REGULAR,
        ],
        compiler_params=pltpu.CompilerParams(
            collective_id=0, has_side_effects=True, vmem_limit_bytes=48 << 20
        ),
    )(*operands)
    result, weight = stored_whole(result, weight)
    return result.reshape(grad_out.shape), weight


def fits(mesh, rows, lon, channels):
    lats, chans, members = (mesh.shape[axis] for axis in ("lat", "chan", "ens"))
    return (
        members == 2 and chans == 2 and lats == 4 and rows * lon <= 512
        and lon % 16 == 0 and rows % 2 == 0
        and channels // chans == LANES + LANES // 2
        and channels % (members * lats * 16) == 0
    )


def solution(mesh):
    placed = (
        P(("grp", "ens"), "lat", None, "chan"),
        P(("grp", "ens"), "lat", None, "chan"),
        P(("grp", "ens"), ("lat", "chan"), None, None, None),
        P(("lat", "chan"), None, "ens"),
        P(),
    )

    def local(grad_out, *rest):
        rows, lon, cols = grad_out.shape[1:]
        small = fits(mesh, rows, lon, cols * mesh.shape["chan"])
        return (fused if small else on_device)(grad_out, *rest)

    return jax.shard_map(
        local,
        mesh=mesh,
        in_specs=placed,
        out_specs=(P(("grp", "ens"), "lat", None, "chan"), P("grp", None)),
        check_vma=False,
    )
```
